1024 devices in a mesh: gx: 16 (over z_hi, y), gy: 8 (over z_lo, core), gz: 8 (over x).
Axes of the slice: x: 8, y: 8, z: 8 (z_hi: 2, z_lo: 4; z = z_hi * 4 + z_lo), core: 2. Of those that a mesh axis runs over, the one named last changes fastest.
Arguments:
- residual: float32 [128, 256, 1024], P('gx', 'gy', 'gz'), may hold values from -32 to 32
- direction: float32 [128, 256, 1024], P('gx', 'gy', 'gz'), may hold values from -32 to 32
- diagonal: float32 [128, 256, 1024], P('gx', 'gy', 'gz'), may hold values from 0.5 to 2
- recycled: bfloat16 [16, 128, 256, 1024], P(None, 'gx', 'gy', 'gz'), may hold values from -6 to 6
- recycled_images: bfloat16 [16, 128, 256, 1024], P(None, 'gx', 'gy', 'gz'), may hold values from -0.00024414062 to 0.00024414062
- coupling_inverse: float32 [16, 16], replicated, may hold values from -1 to 3, as said below
Outputs:
- solution_delta: float32 [128, 256, 1024], P('gx', 'gy', 'gz')
- new_residual: float32 [128, 256, 1024], P('gx', 'gy', 'gz')
- new_direction: float32 [128, 256, 1024], P('gx', 'gy', 'gz')
The draws below stay inside these ranges and needn't reach their ends.
Inputs may be any that keep to these rules, and one draw needn't show every extreme that they name: `coupling_inverse`: symmetric.
All inputs are finite; a program needn't handle non-finite values.
Results may differ from the reference program's by a relative error of at most 0.0028.
Values sent between devices are 32-bit elements; how exact they have to be, the bound alone decides.
A program may use at most 32 MiB of HBM per device.

```python
import jax
import jax.numpy as jnp
import numpy as np
from jax import lax

S = 4
RECYCLED = 16
BASIS = 9
NX = 128
NY = 256
NZ = 1024


def position_scale():
    along_x = 1.0 + 2.0 * jnp.arange(NX, dtype=jnp.float32) / NX
    along_y = 1.0 + 2.0 * jnp.arange(NY, dtype=jnp.float32) / NY
    along_z = 1.0 + 2.0 * jnp.arange(NZ, dtype=jnp.float32) / NZ
    return jnp.sqrt(along_x[:, None, None] * along_y[None, :, None] * along_z[None, None, :])


def field_draw(key, salt):
    subkey = jax.random.fold_in(key, salt)
    values = jnp.clip(jax.random.normal(subkey, (NX, NY, NZ), jnp.float32), -6.0, 6.0)
    return values * position_scale()


def draw_residual(key, part):
    return field_draw(key, 101)


def draw_direction(key, part):
    return field_draw(key, 202)


def draw_coupling_inverse(key, part):
    first_key = jax.random.fold_in(key, 303)
    second_key = jax.random.fold_in(key, 404)
    leading = jax.random.uniform(first_key, (RECYCLED,), jnp.float32, 0.5, 2.0)
    spread = jnp.clip(jax.random.normal(second_key, (RECYCLED, RECYCLED), jnp.float32), -3.0, 3.0) * 0.08
    return jnp.diag(leading) + spread + spread.T


def block_levels(own_key, extent, cuts, least, high):
    def one(axis_at, blocks):
        steps = jax.random.uniform(jax.random.fold_in(jax.random.fold_in(own_key, 6), axis_at), (blocks,), jnp.float32, least / len(cuts), high / len(cuts))
        return jnp.repeat(jnp.exp(steps), extent[axis_at] // blocks).reshape((-1,) + (1,) * (len(extent) - axis_at - 1))

    loudness = one(*cuts[0])
    for cut in cuts[1:]:
        loudness = loudness * one(*cut)
    return loudness


def centred(rng, shape, scale, limit, split=(), kind=jnp.bfloat16):
    level = block_levels(rng, shape, split, -0.22, 0.18) if split else 1.0
    result = jax.random.normal(rng, shape, jnp.float32) * scale * level
    return jnp.minimum(jnp.maximum(result, -limit), limit).astype(kind)


def setup_inputs(seed: int = 0) -> dict:
    keys = jax.random.split(jax.random.key(seed), 7)
    residual = draw_residual(jax.random.fold_in(keys[6], 71), 0)
    direction = draw_direction(jax.random.fold_in(keys[6], 71), 0)
    diagonal = jnp.clip(0.5 + 1.5 * jax.random.uniform(keys[2], (NX, NY, NZ), jnp.float32) ** block_levels(keys[2], (NX, NY, NZ), ((0, 16), (1, 8), (2, 8)), -0.2, 0.2), 0.5, 2.0)
    recycled = centred(keys[3], (RECYCLED, NX, NY, NZ), 1.0, 6.0, ((1, 16), (2, 8), (3, 8)))
    recycled_images = centred(keys[4], (RECYCLED, NX, NY, NZ), (RECYCLED * NX * NY * NZ) ** -0.5, 0.00024414062, ((1, 16), (2, 8), (3, 8)))
    coupling_inverse = draw_coupling_inverse(jax.random.fold_in(keys[6], 71), 0)
    return {"residual": residual, "direction": direction, "diagonal": diagonal, "recycled": recycled, "recycled_images": recycled_images, "coupling_inverse": coupling_inverse}


center = 7.25
half_width = 6.75


def neighbours_sum(values):
    beside_all = jnp.roll(values, -1, 1) + jnp.roll(values, 1, 1)
    beside_all = beside_all + jnp.roll(values, -1, 2) + jnp.roll(values, 1, 2)
    beside_all = beside_all + jnp.roll(values, -1, 3) + jnp.roll(values, 1, 3)
    return beside_all


def chebyshev_next(current, beside_all, diagonal, earlier):
    mapped = (6.0 + diagonal) * current - beside_all
    scaled = (mapped - center * current) / half_width
    if earlier is None:
        return scaled
    return 2.0 * scaled - earlier


def recurrence_matrix():
    recurrence = np.zeros((BASIS, BASIS), np.float32)
    for offset, length in ((0, S + 1), (S + 1, S)):
        recurrence[offset, offset] = center
        recurrence[offset + 1, offset] = half_width
        for column in range(1, length - 1):
            recurrence[offset + column + 1, offset + column] = half_width / 2
            recurrence[offset + column, offset + column] = center
            recurrence[offset + column - 1, offset + column] = half_width / 2
    return jnp.asarray(recurrence, dtype=jnp.float32)


def coordinates(totals, coupling_inverse):
    precise = lax.Precision.HIGHEST
    gram_block = totals[:BASIS]
    projections = totals[BASIS:]
    recurrence = recurrence_matrix()
    counter = jnp.arange(BASIS)
    residue = (counter == S + 1).astype(jnp.float32)
    search = (counter == 0).astype(jnp.float32)
    update = jnp.zeros((BASIS,), jnp.float32)
    norm_now = jnp.dot(residue, jnp.dot(gram_block, residue, precision=precise), precision=precise)
    for iteration in range(S):
        mapped = jnp.dot(recurrence, search, precision=precise)
        step_size = norm_now / jnp.dot(search, jnp.dot(gram_block, mapped, precision=precise), precision=precise)
        update = update + step_size * search
        residue = residue - step_size * mapped
        norm_next = jnp.dot(residue, jnp.dot(gram_block, residue, precision=precise), precision=precise)
        search = residue + (norm_next / norm_now) * search
        norm_now = norm_next
    weights = jnp.dot(coupling_inverse, jnp.dot(projections, residue, precision=precise), precision=precise)
    return update, residue, search, weights.astype(jnp.bfloat16)


def reference(residual, direction, diagonal, recycled, recycled_images, coupling_inverse):
    precise = lax.Precision.HIGHEST
    current = jnp.stack([direction, residual])
    earlier = None
    search_basis = [direction]
    residue_basis = [residual]
    for iteration in range(S):
        if iteration == S - 1:
            current = current[:1]
            earlier = earlier[:1]
        beside_all = neighbours_sum(current)
        following = chebyshev_next(current, beside_all, diagonal, earlier)
        earlier, current = current, following
        search_basis.append(following[0])
        if following.shape[0] > 1:
            residue_basis.append(following[1])
    basis = jnp.stack(search_basis + residue_basis)
    basis_flat = basis.reshape(BASIS, -1)
    gram_block = lax.dot_general(basis_flat, basis_flat, (((1,), (1,)), ((), ())), precision=precise, preferred_element_type=jnp.float32)
    rounded = basis_flat.astype(jnp.bfloat16)
    images = recycled_images.reshape(RECYCLED, -1)
    projections = lax.dot_general(images, rounded, (((1,), (1,)), ((), ())), preferred_element_type=jnp.float32)
    totals = jnp.concatenate([gram_block, projections], 0)
    update, residue, search, weights = coordinates(totals, coupling_inverse)
    shape = residual.shape
    solution_delta = jnp.dot(update, basis_flat, precision=precise).reshape(shape)
    new_residual = jnp.dot(residue, basis_flat, precision=precise).reshape(shape)
    correction = jnp.dot(weights, recycled.reshape(RECYCLED, -1), preferred_element_type=jnp.float32)
    new_direction = (jnp.dot(search, basis_flat, precision=precise) - correction).reshape(shape)
    return solution_delta, new_residual, new_direction
```

```python
import jax
import jax.numpy as jnp
from jax import lax
from jax.experimental import pallas as pl
from jax.experimental.pallas import tpu as pltpu
from jax.sharding import PartitionSpec as P

S = 4
MESH = pl.DeviceIdType.MESH
LOW = 4
ROW = 16
DIR0, RES0, DIAG, DIR1, DIR2, DIR3, DIR4, RES1, RES2, RES3 = range(10)
BASIS = (DIR0, DIR1, DIR2, DIR3, DIR4, RES0, RES1, RES2, RES3)
NB = 9
NR = 16


def rolled(value, shift, axis):
    size = value.shape[axis]
    shift = shift % size
    return pltpu.roll(value, shift, axis) if shift else value


def kernel(
    dir_h, res_h, diag_h, rec_h, img_h, c_ref,
    out_update, out_residual, out_direction,
    fld, edge, rnd, rec_v, img_v,
    strip, strip_low, strip_high, merged,
    tile_send, tile_low, tile_high,
    sums, buf_zc, buf_y, buf_x,
    local_sem, send_sem, recv_sem, zc_send, zc_recv, y_send, y_recv, x_send, x_recv,
):
    nx, ny, nz = lax.axis_size("gx"), lax.axis_size("gy"), lax.axis_size("gz")
    half = nx // 2
    gx, gy, gz = lax.axis_index("gx"), lax.axis_index("gy"), lax.axis_index("gz")
    col = lax.rem(gx, half)
    block = gx - col
    me_zc = lax.div(gx, half) * ny + gy
    x_up = (lax.rem(gx + 1, nx), gy, gz)
    x_down = (lax.rem(gx + nx - 1, nx), gy, gz)
    y_up = (gx, lax.rem(gy + 1, ny), gz)
    y_down = (gx, lax.rem(gy + ny - 1, ny), gz)
    z_up = (gx, gy, lax.rem(gz + 1, nz))
    z_down = (gx, gy, lax.rem(gz + nz - 1, nz))

    def zc_peer(offset):
        peer = lax.rem(me_zc + offset, 2 * ny)
        return peer, (lax.div(peer, ny) * half + col, lax.rem(peer, ny), gz)

    def y_peer(offset):
        peer = lax.rem(col + offset, half)
        return peer, (block + peer, gy, gz)

    def x_peer(offset):
        peer = lax.rem(gz + offset, nz)
        return peer, (gx, gy, peer)

    sources = (dir_h, res_h, diag_h)
    locals_ = []
    for i, src in enumerate(sources):
        locals_.append(pltpu.make_async_copy(src, fld.at[i, LOW:LOW + 8, ROW:ROW + 32], local_sem.at[i]))
    locals_.append(pltpu.make_async_copy(img_h, img_v, local_sem.at[3]))
    locals_.append(pltpu.make_async_copy(rec_h, rec_v, local_sem.at[4]))
    for copy in locals_:
        copy.start()

    barrier = pltpu.get_barrier_semaphore()
    greeted = [x_up, x_down, y_up, y_down, z_up, z_down]
    greeted += [zc_peer(o)[1] for o in range(1, 2 * ny)]
    greeted += [y_peer(o)[1] for o in range(1, half)]
    greeted += [x_peer(o)[1] for o in range(1, nz)]
    for device in greeted:
        pl.semaphore_signal(barrier, inc=1, device_id=device, device_id_type=MESH)
    pl.semaphore_wait(barrier, len(greeted))

    used = [0]

    def send(src, dst, device):
        i = used[0]
        used[0] += 1
        copy = pltpu.make_async_remote_copy(
            src_ref=src, dst_ref=dst, send_sem=send_sem.at[i], recv_sem=recv_sem.at[i],
            device_id=device, device_id_type=MESH,
        )
        copy.start()
        return copy

    x_copies = []
    for i, (src, depth) in enumerate(zip(sources, (4, 3, 3))):
        x_copies.append(send(src.at[8 - depth:8], fld.at[i, LOW - depth:LOW, ROW:ROW + 32], x_up))
        x_copies.append(send(src.at[0:depth], fld.at[i, LOW + 8:LOW + 8 + depth, ROW:ROW + 32], x_down))
    y_copies = []
    for i, src in enumerate(sources):
        y_copies.append(send(src.at[:, 24:32], fld.at[i, LOW:LOW + 8, ROW - 8:ROW], y_up))
        y_copies.append(send(src.at[:, 0:8], fld.at[i, LOW:LOW + 8, ROW + 32:ROW + 40], y_down))

    for copy in locals_[:3]:
        copy.wait()

    lane8 = lax.broadcasted_iota(jnp.int32, (8, 128), 1)
    group8 = lane8 // 8

    @pl.loop(0, 6)
    def _(n):
        i, h = n // 2, n % 2
        packed = jnp.zeros((8, 128), jnp.float32)
        for q in range(16):
            t, x = q // 4, q % 4
            tile = fld[i, LOW + 4 * h + x, ROW + 8 * t:ROW + 8 * t + 8, :]
            packed = jnp.where(group8 == q, rolled(tile, 4 + 8 * q, 1), packed)
        strip[i, h] = packed

    z_copies = [send(strip, strip_low, z_up), send(strip, strip_high, z_down)]
    for copy in z_copies:
        copy.wait()
    from_low = lane8 % 8 < 4
    for i in range(3):
        for h in range(2):
            merged[i, 1 + h] = jnp.where(from_low, strip_low[i, h], strip_high[i, h])
    x_copies.append(send(merged.at[:, 2], merged.at[:, 0], x_up))
    x_copies.append(send(merged.at[:, 1], merged.at[:, 3], x_down))
    for copy in x_copies:
        copy.wait()

    for i, depth in ((0, 3), (1, 2), (2, 2)):
        for first in (LOW - depth, LOW + 8):
            layers = slice(first, first + depth)
            y_copies.append(send(fld.at[i, layers, ROW + 24:ROW + 32], fld.at[i, layers, ROW - 8:ROW], y_up))
            y_copies.append(send(fld.at[i, layers, ROW:ROW + 8], fld.at[i, layers, ROW + 32:ROW + 40], y_down))
    for i in range(3):
        last = jnp.zeros((8, 128), jnp.float32)
        first = jnp.zeros((8, 128), jnp.float32)
        for b in range(4):
            here = (lane8 // 32) == b
            value = merged[i, b]
            last = jnp.where(here, rolled(value, 32 * b - 96, 1), last)
            first = jnp.where(here, rolled(value, 32 * b, 1), first)
        tile_send[0, i] = last
        tile_send[1, i] = first
    y_copies.append(send(tile_send.at[0], tile_low, y_up))
    y_copies.append(send(tile_send.at[1], tile_high, y_down))

    for i in range(3):
        @pl.loop(0, 4)
        def _(b):
            value = merged[i, b]
            for q in range(16):
                t, x = q // 4, q % 4
                edge[i, 4 * b + x, ROW + 8 * t:ROW + 8 * t + 8, :] = rolled(value, -8 * q - 4, 1)

    for copy in y_copies:
        copy.wait()
    for i in range(3):
        low, high = tile_low[i], tile_high[i]
        for x in range(16):
            edge[i, x, ROW - 8:ROW, :] = rolled(low, -8 * x - 4, 1)
            edge[i, x, ROW + 32:ROW + 40, :] = rolled(high, -8 * x - 4, 1)

    def apply(mine, other, into, current, earlier, first, last, top, bottom):
        lane = lax.broadcasted_iota(jnp.int32, (bottom - top, 128), 1)

        @pl.loop(first, last)
        def _(x):
            centre = mine[current, x, top:bottom, :]
            beside = other[current, x, top:bottom, :]
            total = mine[current, x + 1, top:bottom, :] + mine[current, x - 1, top:bottom, :]
            total = total + mine[current, x, top + 1:bottom + 1, :] + mine[current, x, top - 1:bottom - 1, :]
            total = total + pltpu.roll(jnp.where(lane == 0, beside, centre), 127, 1)
            total = total + pltpu.roll(jnp.where(lane == 127, beside, centre), 1, 1)
            result = (mine[DIAG, x, top:bottom, :] - 1.25) * centre - total
            if earlier is None:
                result = result * (1.0 / 6.75)
            else:
                result = result * (2.0 / 6.75) - mine[earlier, x, top:bottom, :]
            mine[into, x, top:bottom, :] = result

    def advance(into, current, earlier, reach):
        if reach == 0:
            apply(fld, edge, into, current, earlier, LOW, LOW + 8, ROW, ROW + 32)
            return
        apply(fld, edge, into, current, earlier, LOW - reach, LOW + 8 + reach, ROW - 8, ROW + 40)
        wide = reach - 1
        apply(edge, fld, into, current, earlier, LOW - wide, LOW + 8 + wide, ROW - 8, ROW + 40)

    advance(DIR1, DIR0, None, 3)
    advance(RES1, RES0, None, 2)
    advance(DIR2, DIR1, DIR0, 2)
    advance(RES2, RES1, RES0, 1)
    advance(DIR3, DIR2, DIR1, 1)
    advance(RES3, RES2, RES1, 0)
    advance(DIR4, DIR3, DIR2, 0)

    pairs = [(i, j) for i in range(NB) for j in range(i, NB)]
    zero = jnp.zeros((8, 128), jnp.float32)

    def gram_step(n, totals):
        x, row = n // 4, pl.multiple_of((n % 4) * 8, 8)
        values = [fld[p, LOW + x, pl.ds(ROW + row, 8), :] for p in BASIS]
        for j, value in enumerate(values):
            rnd[j, x, pl.ds(row, 8), :] = value.astype(jnp.bfloat16).astype(jnp.float32)
        return tuple(t + values[i] * values[j] for t, (i, j) in zip(totals, pairs))

    totals = lax.fori_loop(0, 32, gram_step, (zero,) * len(pairs))
    sums[...] = jnp.zeros_like(sums)
    for total, (i, j) in zip(totals, pairs):
        row = jnp.sum(total, axis=0, keepdims=True)
        sums[9 * i + j:9 * i + j + 1, :] = row
        if i != j:
            sums[9 * j + i:9 * j + i + 1, :] = row

    locals_[3].wait()

    @pl.loop(0, NR // 2)
    def _(pair):
        def projection_step(n, totals):
            x, row = n // 2, pl.multiple_of((n % 2) * 16, 16)
            images = [img_v[2 * pair + m, x, pl.ds(row, 16), :].astype(jnp.float32) for m in range(2)]
            result = []
            for j in range(NB):
                value = rnd[j, x, pl.ds(row, 16), :]
                for m in range(2):
                    product = images[m] * value
                    result.append(totals[2 * j + m] + (product[:8] + product[8:]))
            return tuple(result)

        totals = lax.fori_loop(0, 16, projection_step, (zero,) * (2 * NB))
        for j in range(NB):
            for m in range(2):
                sums[pl.ds(128 + 16 * j + 2 * pair + m, 1), :] = jnp.sum(totals[2 * j + m], axis=0, keepdims=True)

    packed = lax.dot_general(
        jnp.ones((8, 128), jnp.float32), sums[...], (((1,), (1,)), ((), ())),
        precision=lax.Precision.HIGHEST, preferred_element_type=jnp.float32,
    )
    own = jnp.concatenate([packed[0:1, 128 * g:128 * g + 128] for g in range(4)], axis=0)

    def exchange(value, buf, me, peers, count, sends, recvs):
        buf[pl.ds(me, 1)] = value[None]
        copies = []
        for o in range(1, count):
            _, device = peers(o)
            copy = pltpu.make_async_remote_copy(
                src_ref=buf.at[me], dst_ref=buf.at[me], send_sem=sends.at[o], recv_sem=recvs.at[me],
                device_id=device, device_id_type=MESH,
            )
            copy.start()
            copies.append(copy)
        for o in range(1, count):
            peer, device = peers(o)
            pltpu.make_async_remote_copy(
                src_ref=buf.at[peer], dst_ref=buf.at[peer], send_sem=sends.at[o], recv_sem=recvs.at[peer],
                device_id=device, device_id_type=MESH,
            ).wait_recv()
        for copy in copies:
            copy.wait_send()
        return jnp.sum(buf[...], axis=0)

    own = exchange(own, buf_zc, me_zc, zc_peer, 2 * ny, zc_send, zc_recv)
    own = exchange(own, buf_y, col, y_peer, half, y_send, y_recv)
    own = exchange(own, buf_x, gz, x_peer, nz, x_send, x_recv)

    shape = (16, 128)
    sub = lax.broadcasted_iota(jnp.int32, shape, 0)
    lane = lax.broadcasted_iota(jnp.int32, shape, 1)
    gram = jnp.zeros(shape, jnp.float32)
    for i in range(NB):
        gram = jnp.where(sub == i, jnp.broadcast_to(rolled(own[0:1], -9 * i, 1), shape), gram)
    gram = jnp.where(lane < NB, gram, 0.0)
    proj = jnp.zeros(shape, jnp.float32)
    for j in range(NB):
        proj = jnp.where(sub == j, jnp.broadcast_to(rolled(own[1 + j // 8:2 + j // 8], -16 * j, 1), shape), proj)

    def recurrence(index):
        def among(*which):
            hit = index == which[0]
            for w in which[1:]:
                hit = jnp.logical_or(hit, index == w)
            return hit
        before = jnp.where(among(1, 6), 6.75, jnp.where(among(2, 3, 4, 7, 8), 3.375, 0.0))
        at = jnp.where(among(0, 1, 2, 3, 5, 6, 7), 7.25, 0.0)
        after = jnp.where(among(0, 1, 2, 5, 6), 3.375, 0.0)
        return before, at, after

    coeffs = (recurrence(sub), recurrence(lane))

    def mapped_of(vector, axis):
        before, at, after = coeffs[axis]
        return before * rolled(vector, 1, axis) + at * vector + after * rolled(vector, -1, axis)

    def form(left, right):
        return jnp.broadcast_to(jnp.sum(jnp.sum(gram * left * right, axis=1, keepdims=True), axis=0, keepdims=True), shape)

    residue = [jnp.where(k == S + 1, 1.0, 0.0) for k in (sub, lane)]
    search = [jnp.where(k == 0, 1.0, 0.0) for k in (sub, lane)]
    update = jnp.zeros(shape, jnp.float32)
    norm_now = form(residue[0], residue[1])
    for _ in range(S):
        mapped = [mapped_of(search[a], a) for a in range(2)]
        step = norm_now / form(search[0], mapped[1])
        update = update + step * search[0]
        residue = [residue[a] - step * mapped[a] for a in range(2)]
        norm_next = form(residue[0], residue[1])
        ratio = norm_next / norm_now
        search = [residue[a] + ratio * search[a] for a in range(2)]
        norm_now = norm_next
    inner = jnp.sum(proj * residue[0], axis=0, keepdims=True)
    weights = jnp.sum(c_ref[...] * inner[:, :NR], axis=1, keepdims=True)
    weights = jnp.broadcast_to(weights.astype(jnp.bfloat16).astype(jnp.float32), (NR, 128))

    locals_[4].wait()

    def spread(vector, i):
        return jnp.broadcast_to(vector[i:i + 1, :], (8, 128))

    ups = [spread(update, i) for i in range(NB)]
    ress = [spread(residue[0], i) for i in range(NB)]
    seas = [spread(search[0], i) for i in range(NB)]

    @pl.loop(0, 32)
    def _(n):
        x, row = n // 4, pl.multiple_of((n % 4) * 8, 8)
        u = r = s = None
        for i, p in enumerate(BASIS):
            value = fld[p, LOW + x, pl.ds(ROW + row, 8), :]
            u = ups[i] * value if u is None else u + ups[i] * value
            r = ress[i] * value if r is None else r + ress[i] * value
            s = seas[i] * value if s is None else s + seas[i] * value
        out_update[x, pl.ds(row, 8), :] = u
        out_residual[x, pl.ds(row, 8), :] = r
        out_direction[x, pl.ds(row, 8), :] = s

    ws = [jnp.broadcast_to(weights[k:k + 1, :], (16, 128)) for k in range(NR)]

    @pl.loop(0, 16)
    def _(n):
        x, row = n // 2, pl.multiple_of((n % 2) * 16, 16)
        total = None
        for k in range(NR):
            term = ws[k] * rec_v[k, x, pl.ds(row, 16), :].astype(jnp.float32)
            total = term if total is None else total + term
        out_direction[x, pl.ds(row, 16), :] = out_direction[x, pl.ds(row, 16), :] - total


def body(residual, direction, diagonal, recycled, recycled_images, coupling_inverse):
    f32 = jnp.float32
    ny, nz = lax.axis_size("gy"), lax.axis_size("gz")
    half = lax.axis_size("gx") // 2
    anywhere = pl.BlockSpec(memory_space=pl.ANY)
    vmem = pl.BlockSpec(memory_space=pltpu.VMEM)
    tile = (8, 128)
    copies = 48
    return pl.pallas_call(
        kernel,
        out_shape=[jax.ShapeDtypeStruct(residual.shape, f32)] * 3,
        in_specs=[anywhere] * 5 + [vmem],
        out_specs=[vmem] * 3,
        scratch_shapes=[
            pltpu.VMEM((10, 16, 64, 128), f32),
            pltpu.VMEM((10, 16, 64, 128), f32),
            pltpu.VMEM((NB, 8, 32, 128), f32),
            pltpu.VMEM(recycled.shape, jnp.bfloat16),
            pltpu.VMEM(recycled.shape, jnp.bfloat16),
            pltpu.VMEM((3, 2) + tile, f32),
            pltpu.VMEM((3, 2) + tile, f32),
            pltpu.VMEM((3, 2) + tile, f32),
            pltpu.VMEM((3, 4) + tile, f32),
            pltpu.VMEM((2, 3) + tile, f32),
            pltpu.VMEM((3,) + tile, f32),
            pltpu.VMEM((3,) + tile, f32),
            pltpu.VMEM((512, 128), f32),
            pltpu.VMEM((2 * ny, 4, 128), f32),
            pltpu.VMEM((half, 4, 128), f32),
            pltpu.VMEM((nz, 4, 128), f32),
            pltpu.SemaphoreType.DMA((5,)),
            pltpu.SemaphoreType.DMA((copies,)),
            pltpu.SemaphoreType.DMA((copies,)),
            pltpu.SemaphoreType.DMA((2 * ny,)),
            pltpu.SemaphoreType.DMA((2 * ny,)),
            pltpu.SemaphoreType.DMA((half,)),
            pltpu.SemaphoreType.DMA((half,)),
            pltpu.SemaphoreType.DMA((nz,)),
            pltpu.SemaphoreType.DMA((nz,)),
        ],
        compiler_params=pltpu.CompilerParams(collective_id=0, has_side_effects=True),
        name="block",
    )(direction, residual, diagonal, recycled, recycled_images, coupling_inverse)


def solution(mesh):
    field = P("gx", "gy", "gz")
    many = P(None, "gx", "gy", "gz")
    return jax.shard_map(
        body, mesh=mesh,
        in_specs=(field, field, field, many, many, P()),
        out_specs=(field, field, field),
        check_vma=False,
    )
```

```python
import jax
import jax.numpy as jnp
from jax import lax
from jax.experimental import pallas as pl
from jax.experimental.pallas import tpu as pltpu
from jax.sharding import PartitionSpec as P

S = 4
MESH = pl.DeviceIdType.MESH
LOW = 4
ROW = 16
DIR0, RES0, DIAG, DIR1, DIR2, DIR3, DIR4, RES1, RES2, RES3 = range(10)
BASIS = (DIR0, DIR1, DIR2, DIR3, DIR4, RES0, RES1, RES2, RES3)
NB = 9
NR = 16


def rolled(value, shift, axis):
    size = value.shape[axis]
    shift = shift % size
    return pltpu.roll(value, shift, axis) if shift else value


def kernel(
    dir_h, res_h, diag_h, img_h, c_ref,
    basis_out, coord_out,
    fld, edge, rnd, img_v,
    strip, strip_low, strip_high, merged,
    tile_send, tile_low, tile_high,
    sums, buf_zc, buf_y, buf_x,
    local_sem, out_sem, send_sem, recv_sem, zc_send, zc_recv, y_send, y_recv, x_send, x_recv,
):
    nx, ny, nz = lax.axis_size("gx"), lax.axis_size("gy"), lax.axis_size("gz")
    half = nx // 2
    gx, gy, gz = lax.axis_index("gx"), lax.axis_index("gy"), lax.axis_index("gz")
    col = lax.rem(gx, half)
    block = gx - col
    me_zc = lax.div(gx, half) * ny + gy
    x_up = (lax.rem(gx + 1, nx), gy, gz)
    x_down = (lax.rem(gx + nx - 1, nx), gy, gz)
    y_up = (gx, lax.rem(gy + 1, ny), gz)
    y_down = (gx, lax.rem(gy + ny - 1, ny), gz)
    z_up = (gx, gy, lax.rem(gz + 1, nz))
    z_down = (gx, gy, lax.rem(gz + nz - 1, nz))

    def zc_peer(offset):
        peer = lax.rem(me_zc + offset, 2 * ny)
        return peer, (lax.div(peer, ny) * half + col, lax.rem(peer, ny), gz)

    def y_peer(offset):
        peer = lax.rem(col + offset, half)
        return peer, (block + peer, gy, gz)

    def x_peer(offset):
        peer = lax.rem(gz + offset, nz)
        return peer, (gx, gy, peer)

    sources = (dir_h, res_h, diag_h)
    locals_ = []
    for i, src in enumerate(sources):
        locals_.append(pltpu.make_async_copy(src, fld.at[i, LOW:LOW + 8, ROW:ROW + 32], local_sem.at[i]))
    locals_.append(pltpu.make_async_copy(img_h, img_v, local_sem.at[3]))
    for copy in locals_:
        copy.start()

    barrier = pltpu.get_barrier_semaphore()
    greeted = [x_up, x_down, y_up, y_down, z_up, z_down]
    greeted += [zc_peer(o)[1] for o in range(1, 2 * ny)]
    greeted += [y_peer(o)[1] for o in range(1, half)]
    greeted += [x_peer(o)[1] for o in range(1, nz)]
    for device in greeted:
        pl.semaphore_signal(barrier, inc=1, device_id=device, device_id_type=MESH)
    pl.semaphore_wait(barrier, len(greeted))

    used = [0]

    def send(src, dst, device):
        i = used[0]
        used[0] += 1
        copy = pltpu.make_async_remote_copy(
            src_ref=src, dst_ref=dst, send_sem=send_sem.at[i], recv_sem=recv_sem.at[i],
            device_id=device, device_id_type=MESH,
        )
        copy.start()
        return copy

    x_copies = []
    for i, (src, depth) in enumerate(zip(sources, (4, 3, 3))):
        x_copies.append(send(src.at[8 - depth:8], fld.at[i, LOW - depth:LOW, ROW:ROW + 32], x_up))
        x_copies.append(send(src.at[0:depth], fld.at[i, LOW + 8:LOW + 8 + depth, ROW:ROW + 32], x_down))
    y_copies = []
    for i, src in enumerate(sources):
        y_copies.append(send(src.at[:, 24:32], fld.at[i, LOW:LOW + 8, ROW - 8:ROW], y_up))
        y_copies.append(send(src.at[:, 0:8], fld.at[i, LOW:LOW + 8, ROW + 32:ROW + 40], y_down))

    for copy in locals_[:3]:
        copy.wait()

    lane8 = lax.broadcasted_iota(jnp.int32, (8, 128), 1)
    group8 = lane8 // 8

    for i in range(3):
        for h in range(2):
            packed = jnp.zeros((8, 128), jnp.float32)
            for q in range(16):
                t, x = q // 4, q % 4
                tile = fld[i, LOW + 4 * h + x, ROW + 8 * t:ROW + 8 * t + 8, :]
                packed = jnp.where(group8 == q, rolled(tile, 4 + 8 * q, 1), packed)
            strip[i, h] = packed

    z_copies = [send(strip, strip_low, z_up), send(strip, strip_high, z_down)]
    for copy in z_copies:
        copy.wait()
    from_low = lane8 % 8 < 4
    for i in range(3):
        for h in range(2):
            merged[i, 1 + h] = jnp.where(from_low, strip_low[i, h], strip_high[i, h])
    x_copies.append(send(merged.at[:, 2], merged.at[:, 0], x_up))
    x_copies.append(send(merged.at[:, 1], merged.at[:, 3], x_down))

    def place(b):
        for i in range(3):
            value = merged[i, b]
            for q in range(16):
                t, x = q // 4, q % 4
                edge[i, 4 * b + x, ROW + 8 * t:ROW + 8 * t + 8, :] = rolled(value, -8 * q - 4, 1)

    place(1)
    place(2)
    for copy in x_copies:
        copy.wait()

    for i, depth in ((0, 3), (1, 2), (2, 2)):
        for first in (LOW - depth, LOW + 8):
            layers = slice(first, first + depth)
            y_copies.append(send(fld.at[i, layers, ROW + 24:ROW + 32], fld.at[i, layers, ROW - 8:ROW], y_up))
            y_copies.append(send(fld.at[i, layers, ROW:ROW + 8], fld.at[i, layers, ROW + 32:ROW + 40], y_down))
    for i in range(3):
        last = jnp.zeros((8, 128), jnp.float32)
        first = jnp.zeros((8, 128), jnp.float32)
        for b in range(4):
            here = (lane8 // 32) == b
            value = merged[i, b]
            last = jnp.where(here, rolled(value, 32 * b - 96, 1), last)
            first = jnp.where(here, rolled(value, 32 * b, 1), first)
        tile_send[0, i] = last
        tile_send[1, i] = first
    y_copies.append(send(tile_send.at[0], tile_low, y_up))
    y_copies.append(send(tile_send.at[1], tile_high, y_down))

    place(0)
    place(3)
    for copy in y_copies:
        copy.wait()
    for i in range(3):
        low, high = tile_low[i], tile_high[i]
        for x in range(16):
            edge[i, x, ROW - 8:ROW, :] = rolled(low, -8 * x - 4, 1)
            edge[i, x, ROW + 32:ROW + 40, :] = rolled(high, -8 * x - 4, 1)

    def apply(mine, other, into, current, earlier, first, last, top, bottom):
        lane = lax.broadcasted_iota(jnp.int32, (bottom - top, 128), 1)

        for x in range(first, last):
            centre = mine[current, x, top:bottom, :]
            beside = other[current, x, top:bottom, :]
            total = mine[current, x + 1, top:bottom, :] + mine[current, x - 1, top:bottom, :]
            total = total + mine[current, x, top + 1:bottom + 1, :] + mine[current, x, top - 1:bottom - 1, :]
            total = total + pltpu.roll(jnp.where(lane == 0, beside, centre), 127, 1)
            total = total + pltpu.roll(jnp.where(lane == 127, beside, centre), 1, 1)
            result = (mine[DIAG, x, top:bottom, :] - 1.25) * centre - total
            if earlier is None:
                result = result * (1.0 / 6.75)
            else:
                result = result * (2.0 / 6.75) - mine[earlier, x, top:bottom, :]
            mine[into, x, top:bottom, :] = result

    def advance(into, current, earlier, reach):
        if reach == 0:
            apply(fld, edge, into, current, earlier, LOW, LOW + 8, ROW, ROW + 32)
            return
        apply(fld, edge, into, current, earlier, LOW - reach, LOW + 8 + reach, ROW - 8, ROW + 40)
        wide = reach - 1
        apply(edge, fld, into, current, earlier, LOW - wide, LOW + 8 + wide, ROW - 8, ROW + 40)

    basis_copies = []

    def put_out(plane):
        j = BASIS.index(plane)
        copy = pltpu.make_async_copy(fld.at[plane, LOW:LOW + 8, ROW:ROW + 32], basis_out.at[j], out_sem.at[j])
        copy.start()
        basis_copies.append(copy)

    put_out(DIR0)
    put_out(RES0)
    advance(DIR1, DIR0, None, 3)
    advance(RES1, RES0, None, 2)
    advance(DIR2, DIR1, DIR0, 2)
    advance(RES2, RES1, RES0, 1)
    advance(DIR3, DIR2, DIR1, 1)
    advance(RES3, RES2, RES1, 0)
    advance(DIR4, DIR3, DIR2, 0)

    for plane in (DIR1, RES1, DIR2, RES2, DIR3, RES3, DIR4):
        put_out(plane)

    sums[...] = jnp.zeros_like(sums)
    zero = jnp.zeros((8, 128), jnp.float32)

    def gram_pass(pairs, store):
        first = pairs[0][0]

        def step(x, totals):
            for t in range(4):
                rows = slice(8 * t, 8 * t + 8)
                values = {j: fld[BASIS[j], LOW + x, ROW + 8 * t:ROW + 8 * t + 8, :] for j in range(first, NB)}
                if store:
                    for j, value in values.items():
                        rnd[j, x, rows, :] = value.astype(jnp.bfloat16).astype(jnp.float32)
                totals = [total + values[i] * values[j] for total, (i, j) in zip(totals, pairs)]
            return tuple(totals)

        totals = lax.fori_loop(0, 8, step, (zero,) * len(pairs))
        for total, (i, j) in zip(totals, pairs):
            row = jnp.sum(total, axis=0, keepdims=True)
            sums[9 * i + j:9 * i + j + 1, :] = row
            if i != j:
                sums[9 * j + i:9 * j + i + 1, :] = row

    gram_pass([(i, j) for i in range(3) for j in range(i, NB)], True)
    gram_pass([(i, j) for i in range(3, NB) for j in range(i, NB)], False)

    locals_[3].wait()

    @pl.loop(0, NR // 2)
    def _(pair):
        def projection_step(n, totals):
            totals = list(totals)
            for k in range(4):
                x, row = 2 * n + k // 2, 16 * (k % 2)
                images = [img_v[2 * pair + m, x, row:row + 16, :].astype(jnp.float32) for m in range(2)]
                for j in range(NB):
                    value = rnd[j, x, row:row + 16, :]
                    for m in range(2):
                        product = images[m] * value
                        totals[2 * j + m] = totals[2 * j + m] + (product[:8] + product[8:])
            return tuple(totals)

        totals = lax.fori_loop(0, 4, projection_step, (zero,) * (2 * NB))
        for j in range(NB):
            for m in range(2):
                sums[pl.ds(128 + 16 * j + 2 * pair + m, 1), :] = jnp.sum(totals[2 * j + m], axis=0, keepdims=True)

    packed = lax.dot_general(
        jnp.ones((8, 128), jnp.float32), sums[...], (((1,), (1,)), ((), ())),
        precision=lax.Precision.HIGHEST, preferred_element_type=jnp.float32,
    )
    own = jnp.concatenate([packed[0:1, 128 * g:128 * g + 128] for g in range(4)], axis=0)

    def exchange(value, buf, me, peers, count, sends, recvs):
        buf[pl.ds(me, 1)] = value[None]
        copies = []
        for o in range(1, count):
            _, device = peers(o)
            copy = pltpu.make_async_remote_copy(
                src_ref=buf.at[me], dst_ref=buf.at[me], send_sem=sends.at[o], recv_sem=recvs.at[me],
                device_id=device, device_id_type=MESH,
            )
            copy.start()
            copies.append(copy)
        for o in range(1, count):
            peer, device = peers(o)
            pltpu.make_async_remote_copy(
                src_ref=buf.at[peer], dst_ref=buf.at[peer], send_sem=sends.at[o], recv_sem=recvs.at[peer],
                device_id=device, device_id_type=MESH,
            ).wait_recv()
        for copy in copies:
            copy.wait_send()
        return jnp.sum(buf[...], axis=0)

    own = exchange(own, buf_zc, me_zc, zc_peer, 2 * ny, zc_send, zc_recv)
    own = exchange(own, buf_y, col, y_peer, half, y_send, y_recv)
    own = exchange(own, buf_x, gz, x_peer, nz, x_send, x_recv)

    shape = (16, 128)
    sub = lax.broadcasted_iota(jnp.int32, shape, 0)
    lane = lax.broadcasted_iota(jnp.int32, shape, 1)
    gram = jnp.zeros(shape, jnp.float32)
    for i in range(NB):
        gram = jnp.where(sub == i, jnp.broadcast_to(rolled(own[0:1], -9 * i, 1), shape), gram)
    gram = jnp.where(lane < NB, gram, 0.0)
    proj = jnp.zeros(shape, jnp.float32)
    for j in range(NB):
        proj = jnp.where(sub == j, jnp.broadcast_to(rolled(own[1 + j // 8:2 + j // 8], -16 * j, 1), shape), proj)

    def among(*which):
        hit = sub == which[0]
        for w in which[1:]:
            hit = jnp.logical_or(hit, sub == w)
        return hit

    before = jnp.where(among(1, 6), 6.75, jnp.where(among(2, 3, 4, 7, 8), 3.375, 0.0))
    at = jnp.where(among(0, 1, 2, 3, 5, 6, 7), 7.25, 0.0)
    after = jnp.where(among(0, 1, 2, 5, 6), 3.375, 0.0)

    def mapped_of(vector):
        return before * rolled(vector, 1, 0) + at * vector + after * rolled(vector, -1, 0)

    def along_rows(value):
        return jnp.broadcast_to(jnp.sum(value, axis=0, keepdims=True), shape)

    def along_lanes(value):
        return jnp.broadcast_to(jnp.sum(value, axis=1, keepdims=True), shape)

    residue = jnp.where(sub == S + 1, 1.0, 0.0)
    search = jnp.where(sub == 0, 1.0, 0.0)
    update = jnp.zeros(shape, jnp.float32)
    gram_residue = along_lanes(jnp.where(lane == S + 1, gram, 0.0))
    norm_now = along_rows(residue * gram_residue)
    for _ in range(S):
        mapped = mapped_of(search)
        gram_mapped = along_lanes(gram * along_rows(jnp.where(sub == lane, mapped, 0.0)))
        step = norm_now / along_rows(search * gram_mapped)
        update = update + step * search
        residue = residue - step * mapped
        gram_residue = gram_residue - step * gram_mapped
        norm_next = along_rows(residue * gram_residue)
        search = residue + (norm_next / norm_now) * search
        norm_now = norm_next
    inner = jnp.sum(proj * residue, axis=0, keepdims=True)
    weights = jnp.sum(c_ref[...] * inner[:, :NR], axis=1, keepdims=True)
    weights = jnp.broadcast_to(weights.astype(jnp.bfloat16).astype(jnp.float32), (NR, 128))
    for n, vector in enumerate((update, residue, search, weights)):
        coord_out[16 * n:16 * n + 16, :] = vector
    for copy in basis_copies:
        copy.wait()


def combine(basis, rec, coord, out_update, out_residual, out_direction):
    def spread(n, i):
        return jnp.broadcast_to(coord[16 * n + i:16 * n + i + 1, :], (8, 128))

    factors = [[spread(n, i) for i in range(NB)] for n in range(3)]
    for x in range(8):
        for t in range(4):
            rows = slice(8 * t, 8 * t + 8)
            totals = [None] * 3
            for i in range(NB):
                value = basis[i, x, rows, :]
                for n in range(3):
                    term = factors[n][i] * value
                    totals[n] = term if i == 0 else totals[n] + term
            out_update[x, rows, :] = totals[0]
            out_residual[x, rows, :] = totals[1]
            out_direction[x, rows, :] = totals[2]
    weights = [jnp.broadcast_to(coord[48 + k:49 + k, :], (16, 128)) for k in range(NR)]
    for x in range(8):
        for t in range(2):
            rows = slice(16 * t, 16 * t + 16)
            total = None
            for k in range(NR):
                term = weights[k] * rec[k, x, rows, :].astype(jnp.float32)
                total = term if k == 0 else total + term
            out_direction[x, rows, :] = out_direction[x, rows, :] - total


def body(residual, direction, diagonal, recycled, recycled_images, coupling_inverse):
    f32 = jnp.float32
    ny, nz = lax.axis_size("gy"), lax.axis_size("gz")
    half = lax.axis_size("gx") // 2
    anywhere = pl.BlockSpec(memory_space=pl.ANY)
    vmem = pl.BlockSpec(memory_space=pltpu.VMEM)
    tile = (8, 128)
    copies = 48
    operands = [
        pltpu.with_memory_space_constraint(x, pltpu.MemorySpace.HBM)
        for x in (direction, residual, diagonal, recycled_images, coupling_inverse)
    ]
    basis, coord = pl.pallas_call(
        kernel,
        out_shape=[jax.ShapeDtypeStruct((NB,) + residual.shape, f32), jax.ShapeDtypeStruct((64, 128), f32)],
        in_specs=[anywhere] * 4 + [vmem],
        out_specs=[anywhere, vmem],
        scratch_shapes=[
            pltpu.VMEM((10, 16, 64, 128), f32),
            pltpu.VMEM((10, 16, 64, 128), f32),
            pltpu.VMEM((NB, 8, 32, 128), f32),
            pltpu.VMEM(recycled.shape, jnp.bfloat16),
            pltpu.VMEM((3, 2) + tile, f32),
            pltpu.VMEM((3, 2) + tile, f32),
            pltpu.VMEM((3, 2) + tile, f32),
            pltpu.VMEM((3, 4) + tile, f32),
            pltpu.VMEM((2, 3) + tile, f32),
            pltpu.VMEM((3,) + tile, f32),
            pltpu.VMEM((3,) + tile, f32),
            pltpu.VMEM((512, 128), f32),
            pltpu.VMEM((2 * ny, 4, 128), f32),
            pltpu.VMEM((half, 4, 128), f32),
            pltpu.VMEM((nz, 4, 128), f32),
            pltpu.SemaphoreType.DMA((4,)),
            pltpu.SemaphoreType.DMA((NB,)),
            pltpu.SemaphoreType.DMA((copies,)),
            pltpu.SemaphoreType.DMA((copies,)),
            pltpu.SemaphoreType.DMA((2 * ny,)),
            pltpu.SemaphoreType.DMA((2 * ny,)),
            pltpu.SemaphoreType.DMA((half,)),
            pltpu.SemaphoreType.DMA((half,)),
            pltpu.SemaphoreType.DMA((nz,)),
            pltpu.SemaphoreType.DMA((nz,)),
        ],
        compiler_params=pltpu.CompilerParams(collective_id=0, has_side_effects=True, vmem_limit_bytes=24 * 2**20),
        name="block",
    )(*operands)
    return pl.pallas_call(
        combine,
        out_shape=[jax.ShapeDtypeStruct(residual.shape, f32)] * 3,
        in_specs=[vmem] * 3,
        out_specs=[vmem] * 3,
        compiler_params=pltpu.CompilerParams(vmem_limit_bytes=16 * 2**20),
        name="combine",
    )(basis, recycled, coord)


def solution(mesh):
    field = P("gx", "gy", "gz")
    many = P(None, "gx", "gy", "gz")
    return jax.shard_map(
        body, mesh=mesh,
        in_specs=(field, field, field, many, many, P()),
        out_specs=(field, field, field),
        check_vma=False,
    )
```

```python
import jax
import jax.numpy as jnp
from jax import lax
from jax.experimental import pallas as pl
from jax.experimental.pallas import tpu as pltpu
from jax.sharding import PartitionSpec as P

S = 4
MESH = pl.DeviceIdType.MESH
LOW = 4
ROW = 16
DIR0, RES0, DIAG, DIR1, DIR2, DIR3, DIR4, RES1, RES2, RES3 = range(10)
BASIS = (DIR0, DIR1, DIR2, DIR3, DIR4, RES0, RES1, RES2, RES3)
NB = 9
NR = 16


CORNER = ((DIR0, 1, 3, 0), (DIR0, 2, 2, 3), (DIR0, 3, 1, 5), (RES0, 1, 2, 6), (RES0, 2, 1, 8), (DIAG, 1, 2, 9), (DIAG, 2, 1, 11))
BORDER_CORNER = ((DIR0, 1, 2, 0), (DIR0, 2, 1, 2), (RES0, 1, 1, 3), (DIAG, 1, 1, 4))


def rolled(value, shift, axis):
    size = value.shape[axis]
    shift = shift % size
    return pltpu.roll(value, shift, axis) if shift else value


def halo(
    dir_h, res_h, diag_h,
    fld, edge,
    strip, strip_low, strip_high, merged,
    tile_send, tile_low, tile_high,
    corner_send, corner_recv, border_send, border_recv,
    local_sem, send_sem, recv_sem,
):
    nx, ny, nz = lax.axis_size("gx"), lax.axis_size("gy"), lax.axis_size("gz")
    gx, gy, gz = lax.axis_index("gx"), lax.axis_index("gy"), lax.axis_index("gz")
    x_up = (lax.rem(gx + 1, nx), gy, gz)
    x_down = (lax.rem(gx + nx - 1, nx), gy, gz)
    y_up = (gx, lax.rem(gy + 1, ny), gz)
    y_down = (gx, lax.rem(gy + ny - 1, ny), gz)
    z_up = (gx, gy, lax.rem(gz + 1, nz))
    z_down = (gx, gy, lax.rem(gz + nz - 1, nz))

    corners = [(a, b) for a in (1, -1) for b in (1, -1)]

    def beside(a, b):
        return (lax.rem(gx + a + nx, nx), lax.rem(gy + b + ny, ny), gz)

    sources = (dir_h, res_h, diag_h)
    locals_ = []
    for i, src in enumerate(sources):
        locals_.append(pltpu.make_async_copy(src, fld.at[i, LOW:LOW + 8, ROW:ROW + 32], local_sem.at[i]))
    for copy in locals_:
        copy.start()

    barrier = pltpu.get_barrier_semaphore()
    greeted = [x_up, x_down, y_up, y_down, z_up, z_down] + [beside(a, b) for a, b in corners]
    for device in greeted:
        pl.semaphore_signal(barrier, inc=1, device_id=device, device_id_type=MESH)
    pl.semaphore_wait(barrier, len(greeted))

    used = [0]

    def send(src, dst, device):
        i = used[0]
        used[0] += 1
        copy = pltpu.make_async_remote_copy(
            src_ref=src, dst_ref=dst, send_sem=send_sem.at[i], recv_sem=recv_sem.at[i],
            device_id=device, device_id_type=MESH,
        )
        copy.start()
        return copy

    x_copies = []
    for i, (src, depth) in enumerate(zip(sources, (4, 3, 3))):
        x_copies.append(send(src.at[8 - depth:8], fld.at[i, LOW - depth:LOW, ROW:ROW + 32], x_up))
        x_copies.append(send(src.at[0:depth], fld.at[i, LOW + 8:LOW + 8 + depth, ROW:ROW + 32], x_down))
    y_copies = []
    for i, src in enumerate(sources):
        y_copies.append(send(src.at[:, 24:32], fld.at[i, LOW:LOW + 8, ROW - 8:ROW], y_up))
        y_copies.append(send(src.at[:, 0:8], fld.at[i, LOW:LOW + 8, ROW + 32:ROW + 40], y_down))

    for copy in locals_:
        copy.wait()

    def pack_corner(ref, parts, a, b, tile, n):
        for plane, out, rows, at in parts:
            x = LOW + 8 - out if a == 1 else LOW + out - 1
            y = ROW + 32 - rows if b == 1 else ROW
            tile[n, at:at + rows, :] = ref[plane, x, y:y + rows, :]

    def unpack_corner(ref, parts, a, b, tile, n):
        for plane, out, rows, at in parts:
            x = LOW - out if a == 1 else LOW + 7 + out
            y = ROW - rows if b == 1 else ROW + 32
            ref[plane, x, y:y + rows, :] = tile[n, at:at + rows, :]

    for n, (a, b) in enumerate(corners):
        pack_corner(fld, CORNER, a, b, corner_send, n)
    corner_copies = [send(corner_send.at[n], corner_recv.at[n], beside(a, b)) for n, (a, b) in enumerate(corners)]

    lane8 = lax.broadcasted_iota(jnp.int32, (8, 128), 1)
    group8 = lane8 // 8

    for i in range(3):
        for h in range(2):
            packed = jnp.zeros((8, 128), jnp.float32)
            for q in range(16):
                t, x = q // 4, q % 4
                tile = fld[i, LOW + 4 * h + x, ROW + 8 * t:ROW + 8 * t + 8, :]
                packed = jnp.where(group8 == q, rolled(tile, 4 + 8 * q, 1), packed)
            strip[i, h] = packed

    z_copies = [send(strip, strip_low, z_up), send(strip, strip_high, z_down)]
    for copy in z_copies:
        copy.wait()
    from_low = lane8 % 8 < 4
    for i in range(3):
        for h in range(2):
            merged[i, 1 + h] = jnp.where(from_low, strip_low[i, h], strip_high[i, h])
    x_copies.append(send(merged.at[:, 2], merged.at[:, 0], x_up))
    x_copies.append(send(merged.at[:, 1], merged.at[:, 3], x_down))

    for i in range(3):
        last = jnp.zeros((8, 128), jnp.float32)
        first = jnp.zeros((8, 128), jnp.float32)
        for b in range(1, 3):
            here = (lane8 // 32) == b
            value = merged[i, b]
            last = jnp.where(here, rolled(value, 32 * b - 96, 1), last)
            first = jnp.where(here, rolled(value, 32 * b, 1), first)
        tile_send[0, i] = last
        tile_send[1, i] = first
    y_copies.append(send(tile_send.at[0], tile_low, y_up))
    y_copies.append(send(tile_send.at[1], tile_high, y_down))

    def place(b):
        for i in range(3):
            value = merged[i, b]
            for q in range(16):
                t, x = q // 4, q % 4
                edge[i, 4 * b + x, ROW + 8 * t:ROW + 8 * t + 8, :] = rolled(value, -8 * q - 4, 1)

    place(1)
    place(2)
    for n, (a, b) in enumerate(corners):
        pack_corner(edge, BORDER_CORNER, a, b, border_send, n)
    border_copies = [send(border_send.at[n], border_recv.at[n], beside(a, b)) for n, (a, b) in enumerate(corners)]

    for copy in y_copies:
        copy.wait()
    for i in range(3):
        low, high = tile_low[i], tile_high[i]
        for x in range(4, 12):
            edge[i, x, ROW - 8:ROW, :] = rolled(low, -8 * x - 4, 1)
            edge[i, x, ROW + 32:ROW + 40, :] = rolled(high, -8 * x - 4, 1)
    for copy in x_copies:
        copy.wait()
    place(0)
    place(3)
    for copy in corner_copies + border_copies:
        copy.wait()
    for n, (a, b) in enumerate(corners):
        unpack_corner(fld, CORNER, a, b, corner_recv, n)
        unpack_corner(edge, BORDER_CORNER, a, b, border_recv, n)


def block(
    fld_in, edge_in, img_h, c_ref,
    basis_out, coord_out,
    fld_new, edge_new, rnd, img_v,
    sums, buf_zc, buf_y, buf_x,
    local_sem, out_sem, zc_send, zc_recv, y_send, y_recv, x_send, x_recv,
):
    nx, ny, nz = lax.axis_size("gx"), lax.axis_size("gy"), lax.axis_size("gz")
    half = nx // 2
    gx, gy, gz = lax.axis_index("gx"), lax.axis_index("gy"), lax.axis_index("gz")
    col = lax.rem(gx, half)
    first_col = gx - col
    me_zc = lax.div(gx, half) * ny + gy

    def zc_peer(offset):
        peer = lax.rem(me_zc + offset, 2 * ny)
        return peer, (lax.div(peer, ny) * half + col, lax.rem(peer, ny), gz)

    def y_peer(offset):
        peer = lax.rem(col + offset, half)
        return peer, (first_col + peer, gy, gz)

    def x_peer(offset):
        peer = lax.rem(gz + offset, nz)
        return peer, (gx, gy, peer)

    barrier = pltpu.get_barrier_semaphore()
    greeted = [zc_peer(o)[1] for o in range(1, 2 * ny)]
    greeted += [y_peer(o)[1] for o in range(1, half)]
    greeted += [x_peer(o)[1] for o in range(1, nz)]
    for device in greeted:
        pl.semaphore_signal(barrier, inc=1, device_id=device, device_id_type=MESH)
    images_copy = pltpu.make_async_copy(img_h, img_v, local_sem.at[0])
    images_copy.start()

    class Planes:
        def __init__(self, given, new):
            self.given, self.new = given, new

        def of(self, plane):
            return (self.given, plane) if plane < 3 else (self.new, plane - 3)

        def __getitem__(self, index):
            ref, plane = self.of(index[0])
            return ref[(plane,) + index[1:]]

        def __setitem__(self, index, value):
            ref, plane = self.of(index[0])
            ref[(plane,) + index[1:]] = value

        def own(self, plane):
            ref, plane = self.of(plane)
            return ref.at[plane, LOW:LOW + 8, ROW:ROW + 32]

    fld, edge = Planes(fld_in, fld_new), Planes(edge_in, edge_new)

    def apply(mine, other, into, current, earlier, first, last, top, bottom):
        lane = lax.broadcasted_iota(jnp.int32, (bottom - top, 128), 1)

        for x in range(first, last):
            centre = mine[current, x, top:bottom, :]
            beside = other[current, x, top:bottom, :]
            total = mine[current, x + 1, top:bottom, :] + mine[current, x - 1, top:bottom, :]
            total = total + mine[current, x, top + 1:bottom + 1, :] + mine[current, x, top - 1:bottom - 1, :]
            total = total + pltpu.roll(jnp.where(lane == 0, beside, centre), 127, 1)
            total = total + pltpu.roll(jnp.where(lane == 127, beside, centre), 1, 1)
            result = (mine[DIAG, x, top:bottom, :] - 1.25) * centre - total
            if earlier is None:
                result = result * (1.0 / 6.75)
            else:
                result = result * (2.0 / 6.75) - mine[earlier, x, top:bottom, :]
            mine[into, x, top:bottom, :] = result

    def advance(into, current, earlier, reach):
        if reach == 0:
            apply(fld, edge, into, current, earlier, LOW, LOW + 8, ROW, ROW + 32)
            return
        apply(fld, edge, into, current, earlier, LOW - reach, LOW + 8 + reach, ROW - 8, ROW + 40)
        wide = reach - 1
        apply(edge, fld, into, current, earlier, LOW - wide, LOW + 8 + wide, ROW - 8, ROW + 40)

    basis_copies = []

    def put_out(plane):
        j = BASIS.index(plane)
        copy = pltpu.make_async_copy(fld.own(plane), basis_out.at[j], out_sem.at[j])
        copy.start()
        basis_copies.append(copy)

    put_out(DIR0)
    put_out(RES0)
    advance(DIR1, DIR0, None, 3)
    advance(RES1, RES0, None, 2)
    advance(DIR2, DIR1, DIR0, 2)
    advance(RES2, RES1, RES0, 1)
    advance(DIR3, DIR2, DIR1, 1)
    advance(RES3, RES2, RES1, 0)
    advance(DIR4, DIR3, DIR2, 0)

    for plane in (DIR1, RES1, DIR2, RES2, DIR3, RES3, DIR4):
        put_out(plane)

    sums[...] = jnp.zeros_like(sums)
    zero = jnp.zeros((8, 128), jnp.float32)

    def gram_pass(pairs, store):
        first = pairs[0][0]

        def step(x, totals):
            for t in range(4):
                rows = slice(8 * t, 8 * t + 8)
                values = {j: fld[BASIS[j], LOW + x, ROW + 8 * t:ROW + 8 * t + 8, :] for j in range(first, NB)}
                if store:
                    for j, value in values.items():
                        rnd[j, x, rows, :] = value.astype(jnp.bfloat16).astype(jnp.float32)
                totals = [total + values[i] * values[j] for total, (i, j) in zip(totals, pairs)]
            return tuple(totals)

        totals = lax.fori_loop(0, 8, step, (zero,) * len(pairs))
        for total, (i, j) in zip(totals, pairs):
            row = jnp.sum(total, axis=0, keepdims=True)
            sums[9 * i + j:9 * i + j + 1, :] = row
            if i != j:
                sums[9 * j + i:9 * j + i + 1, :] = row

    gram_pass([(i, j) for i in range(3) for j in range(i, NB)], True)
    gram_pass([(i, j) for i in range(3, NB) for j in range(i, NB)], False)

    images_copy.wait()

    @pl.loop(0, NR // 2)
    def _(pair):
        def projection_step(n, totals):
            totals = list(totals)
            for k in range(4):
                x, row = 2 * n + k // 2, 16 * (k % 2)
                images = [img_v[2 * pair + m, x, row:row + 16, :].astype(jnp.float32) for m in range(2)]
                for j in range(NB):
                    value = rnd[j, x, row:row + 16, :]
                    for m in range(2):
                        product = images[m] * value
                        totals[2 * j + m] = totals[2 * j + m] + (product[:8] + product[8:])
            return tuple(totals)

        totals = lax.fori_loop(0, 4, projection_step, (zero,) * (2 * NB))
        for j in range(NB):
            for m in range(2):
                sums[pl.ds((128 + 16 * j if j < 8 else 96) + 2 * pair + m, 1), :] = jnp.sum(totals[2 * j + m], axis=0, keepdims=True)

    packed = lax.dot_general(
        jnp.ones((8, 128), jnp.float32), sums[...], (((1,), (1,)), ((), ())),
        precision=lax.Precision.HIGHEST, preferred_element_type=jnp.float32,
    )
    own = jnp.concatenate([packed[0:1, 128 * g:128 * g + 128] for g in range(2)], axis=0)

    sent = []

    def exchange(value, buf, me, peers, count, sends, recvs):
        buf[pl.ds(me, 1)] = value[None]
        copies = []
        for o in range(1, count):
            _, device = peers(o)
            copy = pltpu.make_async_remote_copy(
                src_ref=buf.at[me], dst_ref=buf.at[me], send_sem=sends.at[o], recv_sem=recvs.at[me],
                device_id=device, device_id_type=MESH,
            )
            copy.start()
            copies.append(copy)
        for o in range(1, count):
            peer, device = peers(o)
            pltpu.make_async_remote_copy(
                src_ref=buf.at[peer], dst_ref=buf.at[peer], send_sem=sends.at[o], recv_sem=recvs.at[peer],
                device_id=device, device_id_type=MESH,
            ).wait_recv()
        sent.extend(copies)
        return jnp.sum(buf[...], axis=0)

    pl.semaphore_wait(barrier, len(greeted))
    own = exchange(own, buf_zc, me_zc, zc_peer, 2 * ny, zc_send, zc_recv)
    own = exchange(own, buf_y, col, y_peer, half, y_send, y_recv)
    own = exchange(own, buf_x, gz, x_peer, nz, x_send, x_recv)

    shape = (16, 128)
    sub = lax.broadcasted_iota(jnp.int32, shape, 0)
    lane = lax.broadcasted_iota(jnp.int32, shape, 1)
    gram = jnp.zeros(shape, jnp.float32)
    for i in range(NB):
        gram = jnp.where(sub == i, jnp.broadcast_to(rolled(own[0:1], -9 * i, 1), shape), gram)
    gram = jnp.where(lane < NB, gram, 0.0)
    proj = jnp.zeros(shape, jnp.float32)
    for j in range(NB):
        proj = jnp.where(sub == j, jnp.broadcast_to(rolled(own[1:2], -16 * j, 1) if j < 8 else rolled(own[0:1], -96, 1), shape), proj)

    def among(*which):
        hit = sub == which[0]
        for w in which[1:]:
            hit = jnp.logical_or(hit, sub == w)
        return hit

    before = jnp.where(among(1, 6), 6.75, jnp.where(among(2, 3, 4, 7, 8), 3.375, 0.0))
    at = jnp.where(among(0, 1, 2, 3, 5, 6, 7), 7.25, 0.0)
    after = jnp.where(among(0, 1, 2, 5, 6), 3.375, 0.0)

    def mapped_of(vector):
        return before * rolled(vector, 1, 0) + at * vector + after * rolled(vector, -1, 0)

    def along_rows(value):
        return jnp.broadcast_to(jnp.sum(value, axis=0, keepdims=True), shape)

    def along_lanes(value):
        return jnp.broadcast_to(jnp.sum(value, axis=1, keepdims=True), shape)

    residue = jnp.where(sub == S + 1, 1.0, 0.0)
    search = jnp.where(sub == 0, 1.0, 0.0)
    update = jnp.zeros(shape, jnp.float32)
    gram_residue = along_lanes(jnp.where(lane == S + 1, gram, 0.0))
    norm_now = along_rows(residue * gram_residue)
    for _ in range(S):
        mapped = mapped_of(search)
        gram_mapped = along_lanes(gram * along_rows(jnp.where(sub == lane, mapped, 0.0)))
        step = norm_now / along_rows(search * gram_mapped)
        update = update + step * search
        residue = residue - step * mapped
        gram_residue = gram_residue - step * gram_mapped
        norm_next = along_rows(residue * gram_residue)
        search = residue + (norm_next / norm_now) * search
        norm_now = norm_next
    inner = jnp.sum(proj * residue, axis=0, keepdims=True)
    weights = jnp.sum(c_ref[...] * inner[:, :NR], axis=1, keepdims=True)
    weights = jnp.broadcast_to(weights.astype(jnp.bfloat16).astype(jnp.float32), (NR, 128))
    for n, vector in enumerate((update, residue, search, weights)):
        coord_out[16 * n:16 * n + 16, :] = vector
    for copy in sent:
        copy.wait_send()
    for copy in basis_copies:
        copy.wait()


def combine(basis, rec, coord, out_update, out_residual, out_direction):
    def spread(n, i):
        return jnp.broadcast_to(coord[16 * n + i:16 * n + i + 1, :], (8, 128))

    factors = [[spread(n, i) for i in range(NB)] for n in range(3)]
    for x in range(8):
        for t in range(4):
            rows = slice(8 * t, 8 * t + 8)
            totals = [None] * 3
            for i in range(NB):
                value = basis[i, x, rows, :]
                for n in range(3):
                    term = factors[n][i] * value
                    totals[n] = term if i == 0 else totals[n] + term
            out_update[x, rows, :] = totals[0]
            out_residual[x, rows, :] = totals[1]
            out_direction[x, rows, :] = totals[2]
    weights = [jnp.broadcast_to(coord[48 + k:49 + k, :], (16, 128)) for k in range(NR)]
    for x in range(8):
        for t in range(2):
            rows = slice(16 * t, 16 * t + 16)
            total = None
            for k in range(NR):
                term = weights[k] * rec[k, x, rows, :].astype(jnp.float32)
                total = term if k == 0 else total + term
            out_direction[x, rows, :] = out_direction[x, rows, :] - total


def body(residual, direction, diagonal, recycled, recycled_images, coupling_inverse):
    f32 = jnp.float32
    ny, nz = lax.axis_size("gy"), lax.axis_size("gz")
    half = lax.axis_size("gx") // 2
    anywhere = pl.BlockSpec(memory_space=pl.ANY)
    vmem = pl.BlockSpec(memory_space=pltpu.VMEM)
    tile = (8, 128)
    copies = 48
    operands = [
        pltpu.with_memory_space_constraint(x, pltpu.MemorySpace.HBM)
        for x in (direction, residual, diagonal, recycled_images, coupling_inverse)
    ]
    fields, borders = pl.pallas_call(
        halo,
        out_shape=[jax.ShapeDtypeStruct((3, 16, 64, 128), f32)] * 2,
        in_specs=[anywhere] * 3,
        out_specs=[vmem] * 2,
        scratch_shapes=[
            pltpu.VMEM((3, 2) + tile, f32),
            pltpu.VMEM((3, 2) + tile, f32),
            pltpu.VMEM((3, 2) + tile, f32),
            pltpu.VMEM((3, 4) + tile, f32),
            pltpu.VMEM((2, 3) + tile, f32),
            pltpu.VMEM((3,) + tile, f32),
            pltpu.VMEM((3,) + tile, f32),
            pltpu.VMEM((4, 16, 128), f32),
            pltpu.VMEM((4, 16, 128), f32),
            pltpu.VMEM((4,) + tile, f32),
            pltpu.VMEM((4,) + tile, f32),
            pltpu.SemaphoreType.DMA((3,)),
            pltpu.SemaphoreType.DMA((copies,)),
            pltpu.SemaphoreType.DMA((copies,)),
        ],
        compiler_params=pltpu.CompilerParams(collective_id=0, has_side_effects=True, vmem_limit_bytes=16 * 2**20),
        name="halo",
    )(*operands[:3])
    basis, coord = pl.pallas_call(
        block,
        out_shape=[jax.ShapeDtypeStruct((NB,) + residual.shape, f32), jax.ShapeDtypeStruct((64, 128), f32)],
        in_specs=[vmem, vmem, anywhere, vmem],
        out_specs=[anywhere, vmem],
        scratch_shapes=[
            pltpu.VMEM((7, 16, 64, 128), f32),
            pltpu.VMEM((7, 16, 64, 128), f32),
            pltpu.VMEM((NB, 8, 32, 128), f32),
            pltpu.VMEM(recycled.shape, jnp.bfloat16),
            pltpu.VMEM((256, 128), f32),
            pltpu.VMEM((2 * ny, 2, 128), f32),
            pltpu.VMEM((half, 2, 128), f32),
            pltpu.VMEM((nz, 2, 128), f32),
            pltpu.SemaphoreType.DMA((1,)),
            pltpu.SemaphoreType.DMA((NB,)),
            pltpu.SemaphoreType.DMA((2 * ny,)),
            pltpu.SemaphoreType.DMA((2 * ny,)),
            pltpu.SemaphoreType.DMA((half,)),
            pltpu.SemaphoreType.DMA((half,)),
            pltpu.SemaphoreType.DMA((nz,)),
            pltpu.SemaphoreType.DMA((nz,)),
        ],
        compiler_params=pltpu.CompilerParams(collective_id=1, has_side_effects=True, vmem_limit_bytes=24 * 2**20),
        name="block",
    )(fields, borders, *operands[3:])
    return pl.pallas_call(
        combine,
        out_shape=[jax.ShapeDtypeStruct(residual.shape, f32)] * 3,
        in_specs=[vmem] * 3,
        out_specs=[vmem] * 3,
        compiler_params=pltpu.CompilerParams(vmem_limit_bytes=16 * 2**20),
        name="combine",
    )(basis, recycled, coord)


def solution(mesh):
    field = P("gx", "gy", "gz")
    many = P(None, "gx", "gy", "gz")
    return jax.shard_map(
        body, mesh=mesh,
        in_specs=(field, field, field, many, many, P()),
        out_specs=(field, field, field),
        check_vma=False,
    )
```

```python
import jax
import jax.numpy as jnp
from jax import lax
from jax.experimental import pallas as pl
from jax.experimental.pallas import tpu as pltpu
from jax.sharding import PartitionSpec as P

S = 4
MESH = pl.DeviceIdType.MESH
LOW = 4
ROW = 16
DIR0, RES0, DIAG, DIR1, DIR2, DIR3, DIR4, RES1, RES2, RES3 = range(10)
BASIS = (DIR0, DIR1, DIR2, DIR3, DIR4, RES0, RES1, RES2, RES3)
NB = 9
NR = 16


CORNER = ((DIR0, 1, 3, 0), (DIR0, 2, 2, 3), (DIR0, 3, 1, 5), (RES0, 1, 2, 6), (RES0, 2, 1, 8), (DIAG, 1, 2, 9), (DIAG, 2, 1, 11))
BORDER_CORNER = ((DIR0, 1, 2, 0), (DIR0, 2, 1, 2), (RES0, 1, 1, 3), (DIAG, 1, 1, 4))


def rolled(value, shift, axis):
    size = value.shape[axis]
    shift = shift % size
    return pltpu.roll(value, shift, axis) if shift else value


def halo(
    dir_h, res_h, diag_h,
    fld, edge,
    strip, strip_low, strip_high, merged,
    tile_send, tile_low, tile_high,
    corner_send, corner_recv, border_send, border_recv, hop,
    local_sem, hop_sem, send_sem, recv_sem,
):
    nx, ny, nz = lax.axis_size("gx"), lax.axis_size("gy"), lax.axis_size("gz")
    gx, gy, gz = lax.axis_index("gx"), lax.axis_index("gy"), lax.axis_index("gz")
    x_up = (lax.rem(gx + 1, nx), gy, gz)
    x_down = (lax.rem(gx + nx - 1, nx), gy, gz)
    y_up = (gx, lax.rem(gy + 1, ny), gz)
    y_down = (gx, lax.rem(gy + ny - 1, ny), gz)
    z_up = (gx, gy, lax.rem(gz + 1, nz))
    z_down = (gx, gy, lax.rem(gz + nz - 1, nz))

    half = nx // 2
    col = lax.rem(gx, half)
    across = half - (gx - col)
    via = (across + jnp.where(col < 2, col + half - 2, col - (half - 2)), gy, gz)
    takes_part = jnp.logical_or(col < 2, col >= half - 2)
    corners = [(a, b) for a in (1, -1) for b in (1, -1)]

    def beside(a, b):
        return (lax.rem(gx + a + nx, nx), lax.rem(gy + b + ny, ny), gz)

    sources = (dir_h, res_h, diag_h)
    locals_ = []
    for i, src in enumerate(sources):
        locals_.append(pltpu.make_async_copy(src, fld.at[i, LOW:LOW + 8, ROW:ROW + 32], local_sem.at[i]))
    for copy in locals_:
        copy.start()

    barrier = pltpu.get_barrier_semaphore()
    greeted = [x_up, x_down, y_up, y_down, z_up, z_down] + [beside(a, b) for a, b in corners]
    for device in greeted:
        pl.semaphore_signal(barrier, inc=1, device_id=device, device_id_type=MESH)

    @pl.when(takes_part)
    def _():
        pl.semaphore_signal(barrier, inc=1, device_id=via, device_id_type=MESH)
        pl.semaphore_wait(barrier, len(greeted) + 1)

    @pl.when(jnp.logical_not(takes_part))
    def _():
        pl.semaphore_wait(barrier, len(greeted))

    used = [0]

    def prepare(src, dst, device):
        i = used[0]
        used[0] += 1
        copy = pltpu.make_async_remote_copy(
            src_ref=src, dst_ref=dst, send_sem=send_sem.at[i], recv_sem=recv_sem.at[i],
            device_id=device, device_id_type=MESH,
        )
        return copy

    def send(src, dst, device):
        copy = prepare(src, dst, device)
        copy.start()
        return copy

    x_copies = []
    passed_on = []
    for sign, layers, into, device in ((1, diag_h.at[5:8], fld.at[DIAG, LOW - 3:LOW, ROW:ROW + 32], x_up),
                                       (-1, diag_h.at[0:3], fld.at[DIAG, LOW + 8:LOW + 11, ROW:ROW + 32], x_down)):
        i = used[0]
        straight = prepare(layers, into, device)
        aside = pltpu.make_async_remote_copy(
            src_ref=layers, dst_ref=hop, send_sem=send_sem.at[i], recv_sem=hop_sem.at[0],
            device_id=via, device_id_type=MESH,
        )
        at_end = col == (half - 1 if sign == 1 else 0)

        @pl.when(at_end)
        def _():
            aside.start()

        @pl.when(jnp.logical_not(at_end))
        def _():
            straight.start()

        onward = pltpu.make_async_remote_copy(
            src_ref=hop, dst_ref=into, send_sem=hop_sem.at[1], recv_sem=recv_sem.at[i],
            device_id=x_down if sign == 1 else x_up, device_id_type=MESH,
        )
        x_copies.append(straight)
        passed_on.append((col == (1 if sign == 1 else half - 2), aside, onward))
    for i, (src, depth) in enumerate(zip(sources, (4, 3))):
        x_copies.append(send(src.at[8 - depth:8], fld.at[i, LOW - depth:LOW, ROW:ROW + 32], x_up))
        x_copies.append(send(src.at[0:depth], fld.at[i, LOW + 8:LOW + 8 + depth, ROW:ROW + 32], x_down))
    y_copies = []
    for i, src in enumerate(sources):
        y_copies.append(send(src.at[:, 24:32], fld.at[i, LOW:LOW + 8, ROW - 8:ROW], y_up))
        y_copies.append(send(src.at[:, 0:8], fld.at[i, LOW:LOW + 8, ROW + 32:ROW + 40], y_down))

    for copy in locals_:
        copy.wait()

    def pack_corner(ref, parts, a, b, tile, n):
        for plane, out, rows, at in parts:
            x = LOW + 8 - out if a == 1 else LOW + out - 1
            y = ROW + 32 - rows if b == 1 else ROW
            tile[n, at:at + rows, :] = ref[plane, x, y:y + rows, :]

    def unpack_corner(ref, parts, a, b, tile, n):
        for plane, out, rows, at in parts:
            x = LOW - out if a == 1 else LOW + 7 + out
            y = ROW - rows if b == 1 else ROW + 32
            ref[plane, x, y:y + rows, :] = tile[n, at:at + rows, :]

    for n, (a, b) in enumerate(corners):
        pack_corner(fld, CORNER, a, b, corner_send, n)
    corner_copies = [send(corner_send.at[n], corner_recv.at[n], beside(a, b)) for n, (a, b) in enumerate(corners)]

    lane8 = lax.broadcasted_iota(jnp.int32, (8, 128), 1)
    group8 = lane8 // 8

    for i in range(3):
        for h in range(2):
            packed = jnp.zeros((8, 128), jnp.float32)
            for q in range(16):
                t, x = q // 4, q % 4
                tile = fld[i, LOW + 4 * h + x, ROW + 8 * t:ROW + 8 * t + 8, :]
                packed = jnp.where(group8 == q, rolled(tile, 4 + 8 * q, 1), packed)
            strip[i, h] = packed

    z_copies = [send(strip, strip_low, z_up), send(strip, strip_high, z_down)]
    for copy in z_copies:
        copy.wait()
    from_low = lane8 % 8 < 4
    for i in range(3):
        for h in range(2):
            merged[i, 1 + h] = jnp.where(from_low, strip_low[i, h], strip_high[i, h])
    x_copies.append(send(merged.at[:, 2], merged.at[:, 0], x_up))
    x_copies.append(send(merged.at[:, 1], merged.at[:, 3], x_down))

    for i in range(3):
        last = jnp.zeros((8, 128), jnp.float32)
        first = jnp.zeros((8, 128), jnp.float32)
        for b in range(1, 3):
            here = (lane8 // 32) == b
            value = merged[i, b]
            last = jnp.where(here, rolled(value, 32 * b - 96, 1), last)
            first = jnp.where(here, rolled(value, 32 * b, 1), first)
        tile_send[0, i] = last
        tile_send[1, i] = first
    y_copies.append(send(tile_send.at[0], tile_low, y_up))
    y_copies.append(send(tile_send.at[1], tile_high, y_down))

    def place(b):
        for i in range(3):
            value = merged[i, b]
            for q in range(16):
                t, x = q // 4, q % 4
                edge[i, 4 * b + x, ROW + 8 * t:ROW + 8 * t + 8, :] = rolled(value, -8 * q - 4, 1)

    place(1)
    place(2)
    for n, (a, b) in enumerate(corners):
        pack_corner(edge, BORDER_CORNER, a, b, border_send, n)
    border_copies = [send(border_send.at[n], border_recv.at[n], beside(a, b)) for n, (a, b) in enumerate(corners)]

    for here, aside, onward in passed_on:
        @pl.when(here)
        def _():
            aside.wait_recv()
            onward.start()

    for copy in y_copies:
        copy.wait()
    for i in range(3):
        low, high = tile_low[i], tile_high[i]
        for x in range(4, 12):
            edge[i, x, ROW - 8:ROW, :] = rolled(low, -8 * x - 4, 1)
            edge[i, x, ROW + 32:ROW + 40, :] = rolled(high, -8 * x - 4, 1)
    for copy in x_copies:
        copy.wait()
    place(0)
    place(3)
    for copy in corner_copies + border_copies:
        copy.wait()
    for here, aside, onward in passed_on:
        @pl.when(here)
        def _():
            onward.wait_send()

    for n, (a, b) in enumerate(corners):
        unpack_corner(fld, CORNER, a, b, corner_recv, n)
        unpack_corner(edge, BORDER_CORNER, a, b, border_recv, n)


def block(
    fld_in, edge_in, img_h, c_ref,
    basis_out, coord_out,
    fld_new, edge_new, rnd, img_v,
    sums, buf_zc, buf_y, buf_x,
    local_sem, out_sem, zc_send, zc_recv, y_send, y_recv, x_send, x_recv,
):
    nx, ny, nz = lax.axis_size("gx"), lax.axis_size("gy"), lax.axis_size("gz")
    half = nx // 2
    gx, gy, gz = lax.axis_index("gx"), lax.axis_index("gy"), lax.axis_index("gz")
    col = lax.rem(gx, half)
    first_col = gx - col
    me_zc = lax.div(gx, half) * ny + gy

    def zc_peer(offset):
        peer = lax.rem(me_zc + offset, 2 * ny)
        return peer, (lax.div(peer, ny) * half + col, lax.rem(peer, ny), gz)

    def y_peer(offset):
        peer = lax.rem(col + offset, half)
        return peer, (first_col + peer, gy, gz)

    def x_peer(offset):
        peer = lax.rem(gz + offset, nz)
        return peer, (gx, gy, peer)

    barrier = pltpu.get_barrier_semaphore()
    greeted = [zc_peer(o)[1] for o in range(1, 2 * ny)]
    greeted += [y_peer(o)[1] for o in range(1, half)]
    greeted += [x_peer(o)[1] for o in range(1, nz)]
    for device in greeted:
        pl.semaphore_signal(barrier, inc=1, device_id=device, device_id_type=MESH)
    images_copy = pltpu.make_async_copy(img_h, img_v, local_sem.at[0])
    images_copy.start()

    class Planes:
        def __init__(self, given, new):
            self.given, self.new = given, new

        def of(self, plane):
            return (self.given, plane) if plane < 3 else (self.new, plane - 3)

        def __getitem__(self, index):
            ref, plane = self.of(index[0])
            return ref[(plane,) + index[1:]]

        def __setitem__(self, index, value):
            ref, plane = self.of(index[0])
            ref[(plane,) + index[1:]] = value

        def own(self, plane):
            ref, plane = self.of(plane)
            return ref.at[plane, LOW:LOW + 8, ROW:ROW + 32]

    fld, edge = Planes(fld_in, fld_new), Planes(edge_in, edge_new)

    def apply(mine, other, into, current, earlier, first, last, top, bottom):
        lane = lax.broadcasted_iota(jnp.int32, (bottom - top, 128), 1)

        for x in range(first, last):
            centre = mine[current, x, top:bottom, :]
            beside = other[current, x, top:bottom, :]
            total = mine[current, x + 1, top:bottom, :] + mine[current, x - 1, top:bottom, :]
            total = total + mine[current, x, top + 1:bottom + 1, :] + mine[current, x, top - 1:bottom - 1, :]
            total = total + pltpu.roll(jnp.where(lane == 0, beside, centre), 127, 1)
            total = total + pltpu.roll(jnp.where(lane == 127, beside, centre), 1, 1)
            result = (mine[DIAG, x, top:bottom, :] - 1.25) * centre - total
            if earlier is None:
                result = result * (1.0 / 6.75)
            else:
                result = result * (2.0 / 6.75) - mine[earlier, x, top:bottom, :]
            mine[into, x, top:bottom, :] = result

    def advance(into, current, earlier, reach):
        if reach == 0:
            apply(fld, edge, into, current, earlier, LOW, LOW + 8, ROW, ROW + 32)
            return
        apply(fld, edge, into, current, earlier, LOW - reach, LOW + 8 + reach, ROW - 8, ROW + 40)
        wide = reach - 1
        apply(edge, fld, into, current, earlier, LOW - wide, LOW + 8 + wide, ROW - 8, ROW + 40)

    basis_copies = []

    def put_out(plane):
        j = BASIS.index(plane)
        copy = pltpu.make_async_copy(fld.own(plane), basis_out.at[j], out_sem.at[j])
        copy.start()
        basis_copies.append(copy)

    put_out(DIR0)
    put_out(RES0)
    advance(DIR1, DIR0, None, 3)
    advance(RES1, RES0, None, 2)
    advance(DIR2, DIR1, DIR0, 2)
    advance(RES2, RES1, RES0, 1)
    advance(DIR3, DIR2, DIR1, 1)
    advance(RES3, RES2, RES1, 0)
    advance(DIR4, DIR3, DIR2, 0)

    for plane in (DIR1, RES1, DIR2, RES2, DIR3, RES3, DIR4):
        put_out(plane)

    sums[...] = jnp.zeros_like(sums)
    zero = jnp.zeros((8, 128), jnp.float32)

    def gram_pass(pairs, store):
        first = pairs[0][0]

        def step(x, totals):
            for t in range(4):
                rows = slice(8 * t, 8 * t + 8)
                values = {j: fld[BASIS[j], LOW + x, ROW + 8 * t:ROW + 8 * t + 8, :] for j in range(first, NB)}
                if store:
                    for j, value in values.items():
                        rnd[j, x, rows, :] = value.astype(jnp.bfloat16).astype(jnp.float32)
                totals = [total + values[i] * values[j] for total, (i, j) in zip(totals, pairs)]
            return tuple(totals)

        totals = lax.fori_loop(0, 8, step, (zero,) * len(pairs))
        for total, (i, j) in zip(totals, pairs):
            row = jnp.sum(total, axis=0, keepdims=True)
            sums[9 * i + j:9 * i + j + 1, :] = row
            if i != j:
                sums[9 * j + i:9 * j + i + 1, :] = row

    gram_pass([(i, j) for i in range(3) for j in range(i, NB)], True)
    gram_pass([(i, j) for i in range(3, NB) for j in range(i, NB)], False)

    images_copy.wait()

    @pl.loop(0, NR // 2)
    def _(pair):
        def projection_step(n, totals):
            totals = list(totals)
            for k in range(4):
                x, row = 2 * n + k // 2, 16 * (k % 2)
                images = [img_v[2 * pair + m, x, row:row + 16, :].astype(jnp.float32) for m in range(2)]
                for j in range(NB):
                    value = rnd[j, x, row:row + 16, :]
                    for m in range(2):
                        product = images[m] * value
                        totals[2 * j + m] = totals[2 * j + m] + (product[:8] + product[8:])
            return tuple(totals)

        totals = lax.fori_loop(0, 4, projection_step, (zero,) * (2 * NB))
        for j in range(NB):
            for m in range(2):
                sums[pl.ds((128 + 16 * j if j < 8 else 96) + 2 * pair + m, 1), :] = jnp.sum(totals[2 * j + m], axis=0, keepdims=True)

    packed = lax.dot_general(
        jnp.ones((8, 128), jnp.float32), sums[...], (((1,), (1,)), ((), ())),
        precision=lax.Precision.HIGHEST, preferred_element_type=jnp.float32,
    )
    own = jnp.concatenate([packed[0:1, 128 * g:128 * g + 128] for g in range(2)], axis=0)

    sent = []

    def exchange(value, buf, me, peers, count, sends, recvs):
        buf[pl.ds(me, 1)] = value[None]
        copies = []
        for o in range(1, count):
            _, device = peers(o)
            copy = pltpu.make_async_remote_copy(
                src_ref=buf.at[me], dst_ref=buf.at[me], send_sem=sends.at[o], recv_sem=recvs.at[me],
                device_id=device, device_id_type=MESH,
            )
            copy.start()
            copies.append(copy)
        for o in range(1, count):
            peer, device = peers(o)
            pltpu.make_async_remote_copy(
                src_ref=buf.at[peer], dst_ref=buf.at[peer], send_sem=sends.at[o], recv_sem=recvs.at[peer],
                device_id=device, device_id_type=MESH,
            ).wait_recv()
        sent.extend(copies)
        return jnp.sum(buf[...], axis=0)

    pl.semaphore_wait(barrier, len(greeted))
    own = exchange(own, buf_zc, me_zc, zc_peer, 2 * ny, zc_send, zc_recv)
    own = exchange(own, buf_y, col, y_peer, half, y_send, y_recv)
    own = exchange(own, buf_x, gz, x_peer, nz, x_send, x_recv)

    shape = (16, 128)
    sub = lax.broadcasted_iota(jnp.int32, shape, 0)
    lane = lax.broadcasted_iota(jnp.int32, shape, 1)
    gram = jnp.zeros(shape, jnp.float32)
    for i in range(NB):
        gram = jnp.where(sub == i, jnp.broadcast_to(rolled(own[0:1], -9 * i, 1), shape), gram)
    gram = jnp.where(lane < NB, gram, 0.0)
    proj = jnp.zeros(shape, jnp.float32)
    for j in range(NB):
        proj = jnp.where(sub == j, jnp.broadcast_to(rolled(own[1:2], -16 * j, 1) if j < 8 else rolled(own[0:1], -96, 1), shape), proj)

    def among(*which):
        hit = sub == which[0]
        for w in which[1:]:
            hit = jnp.logical_or(hit, sub == w)
        return hit

    before = jnp.where(among(1, 6), 6.75, jnp.where(among(2, 3, 4, 7, 8), 3.375, 0.0))
    at = jnp.where(among(0, 1, 2, 3, 5, 6, 7), 7.25, 0.0)
    after = jnp.where(among(0, 1, 2, 5, 6), 3.375, 0.0)

    def mapped_of(vector):
        return before * rolled(vector, 1, 0) + at * vector + after * rolled(vector, -1, 0)

    def along_rows(value):
        return jnp.broadcast_to(jnp.sum(value, axis=0, keepdims=True), shape)

    def along_lanes(value):
        return jnp.broadcast_to(jnp.sum(value, axis=1, keepdims=True), shape)

    residue = jnp.where(sub == S + 1, 1.0, 0.0)
    search = jnp.where(sub == 0, 1.0, 0.0)
    update = jnp.zeros(shape, jnp.float32)
    gram_residue = along_lanes(jnp.where(lane == S + 1, gram, 0.0))
    norm_now = along_rows(residue * gram_residue)
    for _ in range(S):
        mapped = mapped_of(search)
        gram_mapped = along_lanes(gram * along_rows(jnp.where(sub == lane, mapped, 0.0)))
        step = norm_now / along_rows(search * gram_mapped)
        update = update + step * search
        residue = residue - step * mapped
        gram_residue = gram_residue - step * gram_mapped
        norm_next = along_rows(residue * gram_residue)
        search = residue + (norm_next / norm_now) * search
        norm_now = norm_next
    inner = jnp.sum(proj * residue, axis=0, keepdims=True)
    weights = jnp.sum(c_ref[...] * inner[:, :NR], axis=1, keepdims=True)
    weights = jnp.broadcast_to(weights.astype(jnp.bfloat16).astype(jnp.float32), (NR, 128))
    for n, vector in enumerate((update, residue, search, weights)):
        coord_out[16 * n:16 * n + 16, :] = vector
    for copy in sent:
        copy.wait_send()
    for copy in basis_copies:
        copy.wait()


def combine(basis, rec, coord, out_update, out_residual, out_direction):
    def spread(n, i):
        return jnp.broadcast_to(coord[16 * n + i:16 * n + i + 1, :], (8, 128))

    factors = [[spread(n, i) for i in range(NB)] for n in range(3)]
    for x in range(8):
        for t in range(4):
            rows = slice(8 * t, 8 * t + 8)
            totals = [None] * 3
            for i in range(NB):
                value = basis[i, x, rows, :]
                for n in range(3):
                    term = factors[n][i] * value
                    totals[n] = term if i == 0 else totals[n] + term
            out_update[x, rows, :] = totals[0]
            out_residual[x, rows, :] = totals[1]
            out_direction[x, rows, :] = totals[2]
    weights = [jnp.broadcast_to(coord[48 + k:49 + k, :], (16, 128)) for k in range(NR)]
    for x in range(8):
        for t in range(2):
            rows = slice(16 * t, 16 * t + 16)
            total = None
            for k in range(NR):
                term = weights[k] * rec[k, x, rows, :].astype(jnp.float32)
                total = term if k == 0 else total + term
            out_direction[x, rows, :] = out_direction[x, rows, :] - total


def body(residual, direction, diagonal, recycled, recycled_images, coupling_inverse):
    f32 = jnp.float32
    ny, nz = lax.axis_size("gy"), lax.axis_size("gz")
    half = lax.axis_size("gx") // 2
    anywhere = pl.BlockSpec(memory_space=pl.ANY)
    vmem = pl.BlockSpec(memory_space=pltpu.VMEM)
    tile = (8, 128)
    copies = 48
    operands = [
        pltpu.with_memory_space_constraint(x, pltpu.MemorySpace.HBM)
        for x in (direction, residual, diagonal, recycled_images, coupling_inverse)
    ]
    fields, borders = pl.pallas_call(
        halo,
        out_shape=[jax.ShapeDtypeStruct((3, 16, 64, 128), f32)] * 2,
        in_specs=[anywhere] * 3,
        out_specs=[vmem] * 2,
        scratch_shapes=[
            pltpu.VMEM((3, 2) + tile, f32),
            pltpu.VMEM((3, 2) + tile, f32),
            pltpu.VMEM((3, 2) + tile, f32),
            pltpu.VMEM((3, 4) + tile, f32),
            pltpu.VMEM((2, 3) + tile, f32),
            pltpu.VMEM((3,) + tile, f32),
            pltpu.VMEM((3,) + tile, f32),
            pltpu.VMEM((4, 16, 128), f32),
            pltpu.VMEM((4, 16, 128), f32),
            pltpu.VMEM((4,) + tile, f32),
            pltpu.VMEM((4,) + tile, f32),
            pltpu.VMEM((3, 32, 128), f32),
            pltpu.SemaphoreType.DMA((3,)),
            pltpu.SemaphoreType.DMA((2,)),
            pltpu.SemaphoreType.DMA((copies,)),
            pltpu.SemaphoreType.DMA((copies,)),
        ],
        compiler_params=pltpu.CompilerParams(collective_id=0, has_side_effects=True, vmem_limit_bytes=16 * 2**20),
        name="halo",
    )(*operands[:3])
    basis, coord = pl.pallas_call(
        block,
        out_shape=[jax.ShapeDtypeStruct((NB,) + residual.shape, f32), jax.ShapeDtypeStruct((64, 128), f32)],
        in_specs=[vmem, vmem, anywhere, vmem],
        out_specs=[anywhere, vmem],
        scratch_shapes=[
            pltpu.VMEM((7, 16, 64, 128), f32),
            pltpu.VMEM((7, 16, 64, 128), f32),
            pltpu.VMEM((NB, 8, 32, 128), f32),
            pltpu.VMEM(recycled.shape, jnp.bfloat16),
            pltpu.VMEM((256, 128), f32),
            pltpu.VMEM((2 * ny, 2, 128), f32),
            pltpu.VMEM((half, 2, 128), f32),
            pltpu.VMEM((nz, 2, 128), f32),
            pltpu.SemaphoreType.DMA((1,)),
            pltpu.SemaphoreType.DMA((NB,)),
            pltpu.SemaphoreType.DMA((2 * ny,)),
            pltpu.SemaphoreType.DMA((2 * ny,)),
            pltpu.SemaphoreType.DMA((half,)),
            pltpu.SemaphoreType.DMA((half,)),
            pltpu.SemaphoreType.DMA((nz,)),
            pltpu.SemaphoreType.DMA((nz,)),
        ],
        compiler_params=pltpu.CompilerParams(collective_id=1, has_side_effects=True, vmem_limit_bytes=24 * 2**20),
        name="block",
    )(fields, borders, *operands[3:])
    return pl.pallas_call(
        combine,
        out_shape=[jax.ShapeDtypeStruct(residual.shape, f32)] * 3,
        in_specs=[vmem] * 3,
        out_specs=[vmem] * 3,
        compiler_params=pltpu.CompilerParams(vmem_limit_bytes=16 * 2**20),
        name="combine",
    )(basis, recycled, coord)


def solution(mesh):
    field = P("gx", "gy", "gz")
    many = P(None, "gx", "gy", "gz")
    return jax.shard_map(
        body, mesh=mesh,
        in_specs=(field, field, field, many, many, P()),
        out_specs=(field, field, field),
        check_vma=False,
    )
```

```python
import jax
import jax.numpy as jnp
from jax import lax
from jax.experimental import pallas as pl
from jax.experimental.pallas import tpu as pltpu
from jax.sharding import PartitionSpec as P

S = 4
MESH = pl.DeviceIdType.MESH
LOW = 4
ROW = 16
DIR0, RES0, DIAG, DIR1, DIR2, DIR3, DIR4, RES1, RES2, RES3 = range(10)
BASIS = (DIR0, DIR1, DIR2, DIR3, DIR4, RES0, RES1, RES2, RES3)
NB = 9
NR = 16


CORNER = ((DIR0, 1, 3, 0), (DIR0, 2, 2, 3), (DIR0, 3, 1, 5), (RES0, 1, 2, 6), (RES0, 2, 1, 8), (DIAG, 1, 2, 9), (DIAG, 2, 1, 11))
BORDER_CORNER = ((DIR0, 1, 2, 0), (DIR0, 2, 1, 2), (RES0, 1, 1, 3), (DIAG, 1, 1, 4))


def rolled(value, shift, axis):
    size = value.shape[axis]
    shift = shift % size
    return pltpu.roll(value, shift, axis) if shift else value


def halo(
    dir_h, res_h, diag_h,
    fld, edge,
    strip, strip_low, strip_high, merged,
    tile_send, tile_low, tile_high,
    corner_send, corner_recv, border_send, border_recv, hop,
    local_sem, hop_sem, send_sem, recv_sem,
):
    nx, ny, nz = lax.axis_size("gx"), lax.axis_size("gy"), lax.axis_size("gz")
    gx, gy, gz = lax.axis_index("gx"), lax.axis_index("gy"), lax.axis_index("gz")
    x_up = (lax.rem(gx + 1, nx), gy, gz)
    x_down = (lax.rem(gx + nx - 1, nx), gy, gz)
    y_up = (gx, lax.rem(gy + 1, ny), gz)
    y_down = (gx, lax.rem(gy + ny - 1, ny), gz)
    z_up = (gx, gy, lax.rem(gz + 1, nz))
    z_down = (gx, gy, lax.rem(gz + nz - 1, nz))

    half = nx // 2
    col = lax.rem(gx, half)
    across = half - (gx - col)
    via = (across + jnp.where(col < 2, col + half - 2, col - (half - 2)), gy, gz)
    takes_part = jnp.logical_or(col < 2, col >= half - 2)
    corners = [(a, b) for a in (1, -1) for b in (1, -1)]

    def beside(a, b):
        return (lax.rem(gx + a + nx, nx), lax.rem(gy + b + ny, ny), gz)

    sources = (dir_h, res_h, diag_h)
    locals_ = []
    for i, src in enumerate(sources):
        locals_.append(pltpu.make_async_copy(src, fld.at[i, LOW:LOW + 8, ROW:ROW + 32], local_sem.at[i]))
    for copy in locals_:
        copy.start()

    barrier = pltpu.get_barrier_semaphore()
    greeted = [x_up, x_down, y_up, y_down, z_up, z_down] + [beside(a, b) for a, b in corners]
    for device in greeted:
        pl.semaphore_signal(barrier, inc=1, device_id=device, device_id_type=MESH)

    @pl.when(takes_part)
    def _():
        pl.semaphore_signal(barrier, inc=1, device_id=via, device_id_type=MESH)
        pl.semaphore_wait(barrier, len(greeted) + 1)

    @pl.when(jnp.logical_not(takes_part))
    def _():
        pl.semaphore_wait(barrier, len(greeted))

    used = [0]

    def prepare(src, dst, device):
        i = used[0]
        used[0] += 1
        copy = pltpu.make_async_remote_copy(
            src_ref=src, dst_ref=dst, send_sem=send_sem.at[i], recv_sem=recv_sem.at[i],
            device_id=device, device_id_type=MESH,
        )
        return copy

    def send(src, dst, device):
        copy = prepare(src, dst, device)
        copy.start()
        return copy

    x_copies = []
    passed_on = []
    for sign, layers, into, device in ((1, diag_h.at[5:8], fld.at[DIAG, LOW - 3:LOW, ROW:ROW + 32], x_up),
                                       (-1, diag_h.at[0:3], fld.at[DIAG, LOW + 8:LOW + 11, ROW:ROW + 32], x_down)):
        i = used[0]
        straight = prepare(layers, into, device)
        aside = pltpu.make_async_remote_copy(
            src_ref=layers, dst_ref=hop, send_sem=send_sem.at[i], recv_sem=hop_sem.at[0],
            device_id=via, device_id_type=MESH,
        )
        at_end = col == (half - 1 if sign == 1 else 0)

        @pl.when(at_end)
        def _():
            aside.start()

        @pl.when(jnp.logical_not(at_end))
        def _():
            straight.start()

        onward = pltpu.make_async_remote_copy(
            src_ref=hop, dst_ref=into, send_sem=hop_sem.at[1], recv_sem=recv_sem.at[i],
            device_id=x_down if sign == 1 else x_up, device_id_type=MESH,
        )
        x_copies.append(straight)
        passed_on.append((col == (1 if sign == 1 else half - 2), aside, onward))
    for i, (src, depth) in enumerate(zip(sources, (4, 3))):
        x_copies.append(send(src.at[8 - depth:8], fld.at[i, LOW - depth:LOW, ROW:ROW + 32], x_up))
        x_copies.append(send(src.at[0:depth], fld.at[i, LOW + 8:LOW + 8 + depth, ROW:ROW + 32], x_down))
    y_copies = []
    for i, src in enumerate(sources):
        y_copies.append(send(src.at[:, 24:32], fld.at[i, LOW:LOW + 8, ROW - 8:ROW], y_up))
        y_copies.append(send(src.at[:, 0:8], fld.at[i, LOW:LOW + 8, ROW + 32:ROW + 40], y_down))

    for copy in locals_:
        copy.wait()

    def pack_corner(ref, parts, a, b, tile, n):
        for plane, out, rows, at in parts:
            x = LOW + 8 - out if a == 1 else LOW + out - 1
            y = ROW + 32 - rows if b == 1 else ROW
            tile[n, at:at + rows, :] = ref[plane, x, y:y + rows, :]

    def unpack_corner(ref, parts, a, b, tile, n):
        for plane, out, rows, at in parts:
            x = LOW - out if a == 1 else LOW + 7 + out
            y = ROW - rows if b == 1 else ROW + 32
            ref[plane, x, y:y + rows, :] = tile[n, at:at + rows, :]

    lane8 = lax.broadcasted_iota(jnp.int32, (8, 128), 1)
    group8 = lane8 // 8

    for i in range(3):
        for h in range(2):
            packed = jnp.zeros((8, 128), jnp.float32)
            for q in range(16):
                t, x = q // 4, q % 4
                tile = fld[i, LOW + 4 * h + x, ROW + 8 * t:ROW + 8 * t + 8, :]
                packed = jnp.where(group8 == q, rolled(tile, 4 + 8 * q, 1), packed)
            strip[i, h] = packed

    z_copies = [send(strip, strip_low, z_up), send(strip, strip_high, z_down)]
    for n, (a, b) in enumerate(corners):
        pack_corner(fld, CORNER, a, b, corner_send, n)
    corner_copies = [send(corner_send.at[n], corner_recv.at[n], beside(a, b)) for n, (a, b) in enumerate(corners)]
    for copy in z_copies:
        copy.wait()
    from_low = lane8 % 8 < 4
    for i in range(3):
        for h in range(2):
            merged[i, 1 + h] = jnp.where(from_low, strip_low[i, h], strip_high[i, h])
    x_copies.append(send(merged.at[:, 2], merged.at[:, 0], x_up))
    x_copies.append(send(merged.at[:, 1], merged.at[:, 3], x_down))

    for i in range(3):
        last = jnp.zeros((8, 128), jnp.float32)
        first = jnp.zeros((8, 128), jnp.float32)
        for b in range(1, 3):
            here = (lane8 // 32) == b
            value = merged[i, b]
            last = jnp.where(here, rolled(value, 32 * b - 96, 1), last)
            first = jnp.where(here, rolled(value, 32 * b, 1), first)
        tile_send[0, i] = last
        tile_send[1, i] = first
    y_copies.append(send(tile_send.at[0], tile_low, y_up))
    y_copies.append(send(tile_send.at[1], tile_high, y_down))

    def place(b):
        for i in range(3):
            value = merged[i, b]
            for q in range(16):
                t, x = q // 4, q % 4
                edge[i, 4 * b + x, ROW + 8 * t:ROW + 8 * t + 8, :] = rolled(value, -8 * q - 4, 1)

    place(1)
    place(2)
    for n, (a, b) in enumerate(corners):
        pack_corner(edge, BORDER_CORNER, a, b, border_send, n)
    border_copies = [send(border_send.at[n], border_recv.at[n], beside(a, b)) for n, (a, b) in enumerate(corners)]

    for here, aside, onward in passed_on:
        @pl.when(here)
        def _():
            aside.wait_recv()
            onward.start()

    for copy in y_copies:
        copy.wait()
    for i in range(3):
        low, high = tile_low[i], tile_high[i]
        for x in range(4, 12):
            edge[i, x, ROW - 8:ROW, :] = rolled(low, -8 * x - 4, 1)
            edge[i, x, ROW + 32:ROW + 40, :] = rolled(high, -8 * x - 4, 1)
    for copy in x_copies:
        copy.wait()
    place(0)
    place(3)
    for copy in corner_copies + border_copies:
        copy.wait()
    for here, aside, onward in passed_on:
        @pl.when(here)
        def _():
            onward.wait_send()

    for n, (a, b) in enumerate(corners):
        unpack_corner(fld, CORNER, a, b, corner_recv, n)
        unpack_corner(edge, BORDER_CORNER, a, b, border_recv, n)


def block(
    fld_in, edge_in, img_h, c_ref,
    basis_out, coord_out,
    fld_new, edge_new, rnd, img_v,
    sums, buf_zc, buf_y, buf_x,
    local_sem, out_sem, zc_send, zc_recv, y_send, y_recv, x_send, x_recv,
):
    nx, ny, nz = lax.axis_size("gx"), lax.axis_size("gy"), lax.axis_size("gz")
    half = nx // 2
    gx, gy, gz = lax.axis_index("gx"), lax.axis_index("gy"), lax.axis_index("gz")
    col = lax.rem(gx, half)
    first_col = gx - col
    me_zc = lax.div(gx, half) * ny + gy

    def zc_peer(offset):
        peer = lax.rem(me_zc + offset, 2 * ny)
        return peer, (lax.div(peer, ny) * half + col, lax.rem(peer, ny), gz)

    def y_peer(offset):
        peer = lax.rem(col + offset, half)
        return peer, (first_col + peer, gy, gz)

    def x_peer(offset):
        peer = lax.rem(gz + offset, nz)
        return peer, (gx, gy, peer)

    barrier = pltpu.get_barrier_semaphore()
    greeted = [zc_peer(o)[1] for o in range(1, 2 * ny)]
    greeted += [y_peer(o)[1] for o in range(1, half)]
    greeted += [x_peer(o)[1] for o in range(1, nz)]
    for device in greeted:
        pl.semaphore_signal(barrier, inc=1, device_id=device, device_id_type=MESH)
    images_copy = pltpu.make_async_copy(img_h, img_v, local_sem.at[0])
    images_copy.start()

    class Planes:
        def __init__(self, given, new):
            self.given, self.new = given, new

        def of(self, plane):
            return (self.given, plane) if plane < 3 else (self.new, plane - 3)

        def __getitem__(self, index):
            ref, plane = self.of(index[0])
            return ref[(plane,) + index[1:]]

        def __setitem__(self, index, value):
            ref, plane = self.of(index[0])
            ref[(plane,) + index[1:]] = value

        def own(self, plane):
            ref, plane = self.of(plane)
            return ref.at[plane, LOW:LOW + 8, ROW:ROW + 32]

    fld, edge = Planes(fld_in, fld_new), Planes(edge_in, edge_new)

    def apply(mine, other, into, current, earlier, first, last, top, bottom):
        lane = lax.broadcasted_iota(jnp.int32, (bottom - top, 128), 1)

        for x in range(first, last):
            centre = mine[current, x, top:bottom, :]
            beside = other[current, x, top:bottom, :]
            total = mine[current, x + 1, top:bottom, :] + mine[current, x - 1, top:bottom, :]
            total = total + mine[current, x, top + 1:bottom + 1, :] + mine[current, x, top - 1:bottom - 1, :]
            total = total + pltpu.roll(jnp.where(lane == 0, beside, centre), 127, 1)
            total = total + pltpu.roll(jnp.where(lane == 127, beside, centre), 1, 1)
            result = (mine[DIAG, x, top:bottom, :] - 1.25) * centre - total
            if earlier is None:
                result = result * (1.0 / 6.75)
            else:
                result = result * (2.0 / 6.75) - mine[earlier, x, top:bottom, :]
            mine[into, x, top:bottom, :] = result

    def advance(into, current, earlier, reach):
        if reach == 0:
            apply(fld, edge, into, current, earlier, LOW, LOW + 8, ROW, ROW + 32)
            return
        apply(fld, edge, into, current, earlier, LOW - reach, LOW + 8 + reach, ROW - 8, ROW + 40)
        wide = reach - 1
        apply(edge, fld, into, current, earlier, LOW - wide, LOW + 8 + wide, ROW - 8, ROW + 40)

    basis_copies = []

    def put_out(plane):
        j = BASIS.index(plane)
        copy = pltpu.make_async_copy(fld.own(plane), basis_out.at[j], out_sem.at[j])
        copy.start()
        basis_copies.append(copy)

    put_out(DIR0)
    put_out(RES0)
    advance(DIR1, DIR0, None, 3)
    advance(RES1, RES0, None, 2)
    advance(DIR2, DIR1, DIR0, 2)
    advance(RES2, RES1, RES0, 1)
    advance(DIR3, DIR2, DIR1, 1)
    advance(RES3, RES2, RES1, 0)
    advance(DIR4, DIR3, DIR2, 0)

    for plane in (DIR1, RES1, DIR2, RES2, DIR3, RES3, DIR4):
        put_out(plane)

    sums[...] = jnp.zeros_like(sums)
    zero = jnp.zeros((8, 128), jnp.float32)

    def gram_pass(pairs, store):
        first = pairs[0][0]

        def step(x, totals):
            for t in range(4):
                rows = slice(8 * t, 8 * t + 8)
                values = {j: fld[BASIS[j], LOW + x, ROW + 8 * t:ROW + 8 * t + 8, :] for j in range(first, NB)}
                if store:
                    for j, value in values.items():
                        rnd[j, x, rows, :] = value.astype(jnp.bfloat16).astype(jnp.float32)
                totals = [total + values[i] * values[j] for total, (i, j) in zip(totals, pairs)]
            return tuple(totals)

        totals = lax.fori_loop(0, 8, step, (zero,) * len(pairs))
        for total, (i, j) in zip(totals, pairs):
            row = jnp.sum(total, axis=0, keepdims=True)
            sums[9 * i + j:9 * i + j + 1, :] = row
            if i != j:
                sums[9 * j + i:9 * j + i + 1, :] = row

    gram_pass([(i, j) for i in range(3) for j in range(i, NB)], True)
    gram_pass([(i, j) for i in range(3, NB) for j in range(i, NB)], False)

    images_copy.wait()

    @pl.loop(0, NR // 2)
    def _(pair):
        def projection_step(n, totals):
            totals = list(totals)
            for k in range(4):
                x, row = 2 * n + k // 2, 16 * (k % 2)
                images = [img_v[2 * pair + m, x, row:row + 16, :].astype(jnp.float32) for m in range(2)]
                for j in range(NB):
                    value = rnd[j, x, row:row + 16, :]
                    for m in range(2):
                        product = images[m] * value
                        totals[2 * j + m] = totals[2 * j + m] + (product[:8] + product[8:])
            return tuple(totals)

        totals = lax.fori_loop(0, 4, projection_step, (zero,) * (2 * NB))
        for j in range(NB):
            for m in range(2):
                sums[pl.ds((128 + 16 * j if j < 8 else 96) + 2 * pair + m, 1), :] = jnp.sum(totals[2 * j + m], axis=0, keepdims=True)

    packed = lax.dot_general(
        jnp.ones((8, 128), jnp.float32), sums[...], (((1,), (1,)), ((), ())),
        precision=lax.Precision.HIGHEST, preferred_element_type=jnp.float32,
    )
    own = jnp.concatenate([packed[0:1, 128 * g:128 * g + 128] for g in range(2)], axis=0)

    sent = []

    def exchange(value, buf, me, peers, count, sends, recvs):
        buf[pl.ds(me, 1)] = value[None]
        copies = []
        for o in range(1, count):
            _, device = peers(o)
            copy = pltpu.make_async_remote_copy(
                src_ref=buf.at[me], dst_ref=buf.at[me], send_sem=sends.at[o], recv_sem=recvs.at[me],
                device_id=device, device_id_type=MESH,
            )
            copy.start()
            copies.append(copy)
        for o in range(1, count):
            peer, device = peers(o)
            pltpu.make_async_remote_copy(
                src_ref=buf.at[peer], dst_ref=buf.at[peer], send_sem=sends.at[o], recv_sem=recvs.at[peer],
                device_id=device, device_id_type=MESH,
            ).wait_recv()
        sent.extend(copies)
        return jnp.sum(buf[...], axis=0)

    pl.semaphore_wait(barrier, len(greeted))
    own = exchange(own, buf_zc, me_zc, zc_peer, 2 * ny, zc_send, zc_recv)
    own = exchange(own, buf_y, col, y_peer, half, y_send, y_recv)
    own = exchange(own, buf_x, gz, x_peer, nz, x_send, x_recv)

    shape = (16, 128)
    sub = lax.broadcasted_iota(jnp.int32, shape, 0)
    lane = lax.broadcasted_iota(jnp.int32, shape, 1)
    gram = jnp.zeros(shape, jnp.float32)
    for i in range(NB):
        gram = jnp.where(sub == i, jnp.broadcast_to(rolled(own[0:1], -9 * i, 1), shape), gram)
    gram = jnp.where(lane < NB, gram, 0.0)
    proj = jnp.zeros(shape, jnp.float32)
    for j in range(NB):
        proj = jnp.where(sub == j, jnp.broadcast_to(rolled(own[1:2], -16 * j, 1) if j < 8 else rolled(own[0:1], -96, 1), shape), proj)

    def among(*which):
        hit = sub == which[0]
        for w in which[1:]:
            hit = jnp.logical_or(hit, sub == w)
        return hit

    before = jnp.where(among(1, 6), 6.75, jnp.where(among(2, 3, 4, 7, 8), 3.375, 0.0))
    at = jnp.where(among(0, 1, 2, 3, 5, 6, 7), 7.25, 0.0)
    after = jnp.where(among(0, 1, 2, 5, 6), 3.375, 0.0)

    def mapped_of(vector):
        return before * rolled(vector, 1, 0) + at * vector + after * rolled(vector, -1, 0)

    def along_rows(value):
        return jnp.broadcast_to(jnp.sum(value, axis=0, keepdims=True), shape)

    def along_lanes(value):
        return jnp.broadcast_to(jnp.sum(value, axis=1, keepdims=True), shape)

    residue = jnp.where(sub == S + 1, 1.0, 0.0)
    search = jnp.where(sub == 0, 1.0, 0.0)
    update = jnp.zeros(shape, jnp.float32)
    gram_residue = along_lanes(jnp.where(lane == S + 1, gram, 0.0))
    norm_now = along_rows(residue * gram_residue)
    for _ in range(S):
        mapped = mapped_of(search)
        gram_mapped = along_lanes(gram * along_rows(jnp.where(sub == lane, mapped, 0.0)))
        step = norm_now / along_rows(search * gram_mapped)
        update = update + step * search
        residue = residue - step * mapped
        gram_residue = gram_residue - step * gram_mapped
        norm_next = along_rows(residue * gram_residue)
        search = residue + (norm_next / norm_now) * search
        norm_now = norm_next
    inner = jnp.sum(proj * residue, axis=0, keepdims=True)
    weights = jnp.sum(c_ref[...] * inner[:, :NR], axis=1, keepdims=True)
    weights = jnp.broadcast_to(weights.astype(jnp.bfloat16).astype(jnp.float32), (NR, 128))
    for n, vector in enumerate((update, residue, search, weights)):
        coord_out[16 * n:16 * n + 16, :] = vector
    for copy in sent:
        copy.wait_send()
    for copy in basis_copies:
        copy.wait()


def combine(basis, rec, coord, out_update, out_residual, out_direction):
    def spread(n, i):
        return jnp.broadcast_to(coord[16 * n + i:16 * n + i + 1, :], (8, 128))

    factors = [[spread(n, i) for i in range(NB)] for n in range(3)]
    for x in range(8):
        for t in range(4):
            rows = slice(8 * t, 8 * t + 8)
            totals = [None] * 3
            for i in range(NB):
                value = basis[i, x, rows, :]
                for n in range(3):
                    term = factors[n][i] * value
                    totals[n] = term if i == 0 else totals[n] + term
            out_update[x, rows, :] = totals[0]
            out_residual[x, rows, :] = totals[1]
            out_direction[x, rows, :] = totals[2]
    weights = [jnp.broadcast_to(coord[48 + k:49 + k, :], (16, 128)) for k in range(NR)]
    for x in range(8):
        for t in range(2):
            rows = slice(16 * t, 16 * t + 16)
            total = None
            for k in range(NR):
                term = weights[k] * rec[k, x, rows, :].astype(jnp.float32)
                total = term if k == 0 else total + term
            out_direction[x, rows, :] = out_direction[x, rows, :] - total


def body(residual, direction, diagonal, recycled, recycled_images, coupling_inverse):
    f32 = jnp.float32
    ny, nz = lax.axis_size("gy"), lax.axis_size("gz")
    half = lax.axis_size("gx") // 2
    anywhere = pl.BlockSpec(memory_space=pl.ANY)
    vmem = pl.BlockSpec(memory_space=pltpu.VMEM)
    tile = (8, 128)
    copies = 48
    operands = [
        pltpu.with_memory_space_constraint(x, pltpu.MemorySpace.HBM)
        for x in (direction, residual, diagonal, recycled_images, coupling_inverse)
    ]
    fields, borders = pl.pallas_call(
        halo,
        out_shape=[jax.ShapeDtypeStruct((3, 16, 64, 128), f32)] * 2,
        in_specs=[anywhere] * 3,
        out_specs=[vmem] * 2,
        scratch_shapes=[
            pltpu.VMEM((3, 2) + tile, f32),
            pltpu.VMEM((3, 2) + tile, f32),
            pltpu.VMEM((3, 2) + tile, f32),
            pltpu.VMEM((3, 4) + tile, f32),
            pltpu.VMEM((2, 3) + tile, f32),
            pltpu.VMEM((3,) + tile, f32),
            pltpu.VMEM((3,) + tile, f32),
            pltpu.VMEM((4, 16, 128), f32),
            pltpu.VMEM((4, 16, 128), f32),
            pltpu.VMEM((4,) + tile, f32),
            pltpu.VMEM((4,) + tile, f32),
            pltpu.VMEM((3, 32, 128), f32),
            pltpu.SemaphoreType.DMA((3,)),
            pltpu.SemaphoreType.DMA((2,)),
            pltpu.SemaphoreType.DMA((copies,)),
            pltpu.SemaphoreType.DMA((copies,)),
        ],
        compiler_params=pltpu.CompilerParams(collective_id=0, has_side_effects=True, vmem_limit_bytes=16 * 2**20),
        name="halo",
    )(*operands[:3])
    basis, coord = pl.pallas_call(
        block,
        out_shape=[jax.ShapeDtypeStruct((NB,) + residual.shape, f32), jax.ShapeDtypeStruct((64, 128), f32)],
        in_specs=[vmem, vmem, anywhere, vmem],
        out_specs=[anywhere, vmem],
        scratch_shapes=[
            pltpu.VMEM((7, 16, 64, 128), f32),
            pltpu.VMEM((7, 16, 64, 128), f32),
            pltpu.VMEM((NB, 8, 32, 128), f32),
            pltpu.VMEM(recycled.shape, jnp.bfloat16),
            pltpu.VMEM((256, 128), f32),
            pltpu.VMEM((2 * ny, 2, 128), f32),
            pltpu.VMEM((half, 2, 128), f32),
            pltpu.VMEM((nz, 2, 128), f32),
            pltpu.SemaphoreType.DMA((1,)),
            pltpu.SemaphoreType.DMA((NB,)),
            pltpu.SemaphoreType.DMA((2 * ny,)),
            pltpu.SemaphoreType.DMA((2 * ny,)),
            pltpu.SemaphoreType.DMA((half,)),
            pltpu.SemaphoreType.DMA((half,)),
            pltpu.SemaphoreType.DMA((nz,)),
            pltpu.SemaphoreType.DMA((nz,)),
        ],
        compiler_params=pltpu.CompilerParams(collective_id=1, has_side_effects=True, vmem_limit_bytes=24 * 2**20),
        name="block",
    )(fields, borders, *operands[3:])
    return pl.pallas_call(
        combine,
        out_shape=[jax.ShapeDtypeStruct(residual.shape, f32)] * 3,
        in_specs=[vmem] * 3,
        out_specs=[vmem] * 3,
        compiler_params=pltpu.CompilerParams(vmem_limit_bytes=16 * 2**20),
        name="combine",
    )(basis, recycled, coord)


def solution(mesh):
    field = P("gx", "gy", "gz")
    many = P(None, "gx", "gy", "gz")
    return jax.shard_map(
        body, mesh=mesh,
        in_specs=(field, field, field, many, many, P()),
        out_specs=(field, field, field),
        check_vma=False,
    )
```
